512 devices in a mesh: layer: 32 (over y, x), dp: 16 (over z, core).
Axes of the slice: x: 4, y: 8, z: 8, core: 2. Of those that a mesh axis runs over, the one named last changes fastest.
Arguments:
- states: bfloat16 [64, 16, 128, 1024], P('layer', 'dp'), may hold values from -6 to 6
- filters: bfloat16 [64, 128, 1152], P('layer'), may hold values from -0.1875 to 0.1875
- guess_adjoint: bfloat16 [64, 16, 128, 1024], P('layer', 'dp'), may hold values from -4 to 4
- terminal: bfloat16 [16, 128, 1024], P('dp'), may hold values from -6 to 6
Outputs:
- adjoint: bfloat16 [64, 16, 128, 1024], P('layer', 'dp')
- filter_grad: float32 [64, 128, 1152], P('layer', 'dp')
The draws below stay inside these ranges and needn't reach their ends.
All inputs are finite; a program needn't handle non-finite values.
Results may differ from the reference program's by a relative error of at most 0.0057.
Values may be sent and summed in bfloat16 or wider, within the bound.
No kernel may reach another device: no remote copies, remote signals or barrier semaphores. Data moves between devices by JAX's collectives and lax.ppermute only.
A program may use at most 64 MiB of HBM per device.

```python
import math
import jax
import jax.numpy as jnp
from jax import lax

CH = 128
L_DEV = 2
PIX = 1024
LAYERS = 64
IMAGES = 16
N_LAYER = 32


def level_of(own_key, extent, shards, smallest, high):
    loudness = 1.0
    for axis_at, blocks in shards:
        draws = jax.random.uniform(jax.random.fold_in(jax.random.fold_in(own_key, 6), axis_at), (blocks,), jnp.float32, smallest / len(shards), high / len(shards))
        loudness = loudness * jnp.repeat(jnp.exp(draws), extent[axis_at] // blocks).reshape((-1,) + (1,) * (len(extent) - 1 - axis_at))
    return loudness


def gaussian(rng, dims, deviation, reach, split=(), kind=jnp.bfloat16):
    gain = level_of(rng, dims, split, -0.22, 0.18) if split else 1.0
    array = jax.random.normal(rng, dims, jnp.float32) * deviation * gain
    return jnp.minimum(jnp.maximum(array, -reach), reach).astype(kind)


def setup_inputs(seed: int = 0) -> dict:
    splits = jax.random.split(jax.random.key(seed), 5)
    states = gaussian(splits[0], (LAYERS, IMAGES, CH, PIX), 1.0, 6.0, ((0, 32), (1, 16)))
    filters = gaussian(splits[1], (LAYERS, CH, 9 * CH), (9 * CH) ** -0.5, 0.1875, ((0, 32),))
    guess_adjoint = gaussian(splits[2], (LAYERS, IMAGES, CH, PIX), 0.5, 4.0, ((0, 32), (1, 16)))
    terminal = gaussian(splits[3], (IMAGES, CH, PIX), 1.0, 6.0, ((0, 16),))
    return dict(states=states, filters=filters, guess_adjoint=guess_adjoint, terminal=terminal)


step_size = 0.0625

def shifted_stack(in_field):
    images, channels, pixels = in_field.shape
    grid_side = math.isqrt(pixels)
    grid_field = in_field.reshape(images, channels, grid_side, grid_side)
    padded = jnp.pad(grid_field, ((0, 0), (0, 0), (1, 1), (1, 1)))
    pieces = []
    for row_off in (-1, 0, 1):
        for col_off in (-1, 0, 1):
            pieces.append(padded[:, :, 1 - row_off:1 - row_off + grid_side, 1 - col_off:1 - col_off + grid_side])
    return jnp.stack(pieces, axis=1).reshape(images, 9 * channels, pixels)

def adjoint_step(carried, stacked, layer_state, kernel):
    backward = jnp.einsum('ck,bkp->bcp', kernel.astype(jnp.float32), stacked.astype(jnp.float32))
    slope_term = 1.0 - jnp.tanh(layer_state.astype(jnp.float32)) ** 2
    return (1.0 - step_size) * carried.astype(jnp.float32) + step_size * slope_term * backward

def layer_gradient(layer_state, stacked):
    activation = jnp.tanh(layer_state.astype(jnp.float32)).astype(jnp.bfloat16)
    return step_size * jnp.einsum('bcp,bkp->ck', activation.astype(jnp.float32), stacked.astype(jnp.float32))

def pool_field(in_field):
    images, channels, pixels = in_field.shape
    half_side = math.isqrt(pixels) // 2
    grid_field = in_field.reshape(images, channels, half_side, 2, half_side, 2)
    return lax.optimization_barrier(jnp.mean(grid_field, axis=(3, 5))).reshape(images, channels, half_side * half_side)

def spread_field(coarse):
    images, channels, cells = coarse.shape
    half_side = math.isqrt(cells)
    grid_field = coarse.reshape(images, channels, half_side, 1, half_side, 1)
    grid_field = jnp.broadcast_to(grid_field, (images, channels, half_side, 2, half_side, 2))
    return grid_field.reshape(images, channels, 4 * cells)

def coarse_matrix(kernel, window_depth):
    channels = kernel.shape[0]
    summed = lax.optimization_barrier(jnp.sum(kernel.astype(jnp.float32).reshape(channels, 9, channels), axis=1))
    base_matrix = (1.0 - step_size) * jnp.eye(channels, dtype=jnp.float32) + step_size * summed

    def times_base(count_idx, product):
        return jnp.dot(product, base_matrix, precision=lax.Precision.HIGHEST)
    return lax.fori_loop(0, window_depth - 1, times_base, base_matrix)

def apply_matrix(matrix, in_field):
    return jnp.einsum('ij,bjp->bip', matrix, in_field, precision=lax.Precision.HIGHEST)

def fine_sweep(top_adjoint, layer_states, kernels):

    def relax_layer(carried, layer_pair):
        layer_state, kernel = layer_pair
        fresh_adjoint = adjoint_step(carried, shifted_stack(carried), layer_state, kernel).astype(jnp.bfloat16)
        return (fresh_adjoint, None)
    carried, unused = lax.scan(relax_layer, top_adjoint, (layer_states[1:], kernels[1:]), reverse=True)
    return carried

def corrected_sweep(top_adjoint, layer_states, kernels, c_point):

    def relax_layer(carried, layer_pair):
        layer_state, kernel = layer_pair
        stacked = shifted_stack(carried)
        fresh_adjoint = adjoint_step(carried, stacked, layer_state, kernel).astype(jnp.bfloat16)
        return (fresh_adjoint, (fresh_adjoint, layer_gradient(layer_state, stacked)))
    carried, outputs = lax.scan(relax_layer, top_adjoint, (layer_states[1:], kernels[1:]), reverse=True)
    fresh_all, gradients = outputs
    first_grad = layer_gradient(layer_states[0], shifted_stack(carried))
    adjoint_block = jnp.concatenate([c_point[None], fresh_all], axis=0)
    grad_block = jnp.concatenate([first_grad[None], gradients], axis=0)
    return (adjoint_block, grad_block)

def reference(states, filters, guess_adjoint, terminal):
    states_blk = states.reshape((N_LAYER, L_DEV) + states.shape[1:])
    filters_blk = filters.reshape((N_LAYER, L_DEV) + filters.shape[1:])
    guess_blk = guess_adjoint.reshape((N_LAYER, L_DEV) + guess_adjoint.shape[1:])
    tops = jnp.concatenate([guess_blk[1:, 0], terminal[None]], axis=0)

    def phase_one(block_data):
        state_blk, kernel_blk, guess_one, top_adjoint = block_data
        below_adjoint = fine_sweep(top_adjoint, state_blk, kernel_blk)
        residual = adjoint_step(below_adjoint, shifted_stack(below_adjoint), state_blk[0], kernel_blk[0]) - guess_one[0].astype(jnp.float32)
        return (pool_field(residual), coarse_matrix(kernel_blk[0], L_DEV))
    coarse_residual, matrices = lax.map(phase_one, (states_blk, filters_blk, guess_blk, tops))

    def chain_step(chain_carry, layer_pair):
        coarse_map, coarse_one = layer_pair
        fresh_error = apply_matrix(coarse_map, chain_carry) + coarse_one
        return (fresh_error, fresh_error)
    zero_error = jnp.zeros(coarse_residual.shape[1:], jnp.float32)
    unused, errors = lax.scan(chain_step, zero_error, (matrices, coarse_residual), reverse=True)
    above_errors = jnp.concatenate([errors[1:], zero_error[None]], axis=0)

    def phase_two(block_data):
        state_blk, kernel_blk, guess_one, top_adjoint, own_error, upper_error = block_data
        c_point = (guess_one[0].astype(jnp.float32) + spread_field(own_error)).astype(jnp.bfloat16)
        new_top = (top_adjoint.astype(jnp.float32) + spread_field(upper_error)).astype(jnp.bfloat16)
        return corrected_sweep(new_top, state_blk, kernel_blk, c_point)
    adjoint_all, grad_all = lax.map(phase_two, (states_blk, filters_blk, guess_blk, tops, errors, above_errors))
    return (adjoint_all.reshape(states.shape), grad_all.reshape(filters.shape))
```

```python
import functools

import jax
import jax.numpy as jnp
from jax import lax
from jax.experimental import pallas as pl
from jax.experimental.pallas import tpu as pltpu
from jax.sharding import PartitionSpec as P

STEP = 0.0625
KEEP = 1.0 - STEP
SIDE, PIX, CH, TAPS = 32, 1024, 128, 9
HALF = SIDE // 2
CELLS = HALF * HALF
XS, YS, ZS = 4, 8, 8
BF, F32 = jnp.bfloat16, jnp.float32
EXACT = lax.Precision.HIGHEST
VMEM = pl.BlockSpec(memory_space=pltpu.VMEM)


def dot(a, b, precision=None):
    return jnp.dot(a, b, preferred_element_type=F32, precision=precision)


def split(a):
    high = a.astype(BF)
    return high, (a - high.astype(F32)).astype(BF)


def write_stack(field, stack_ref):
    lane = lax.broadcasted_iota(jnp.int32, (1, PIX), 1)
    col = lane & (SIDE - 1)
    first, last = (col != 0).astype(BF), (col != SIDE - 1).astype(BF)
    top, bottom = (lane >= SIDE).astype(BF), (lane < PIX - SIDE).astype(BF)
    columns = (
        pltpu.roll(field, PIX - 1, 1) * last,
        field,
        pltpu.roll(field, 1, 1) * first,
    )
    for c, moved in enumerate(columns):
        rows = (
            pltpu.roll(moved, PIX - SIDE, 1) * bottom,
            moved,
            pltpu.roll(moved, SIDE, 1) * top,
        )
        for a, piece in enumerate(rows):
            t = 3 * a + c
            stack_ref[t * CH : (t + 1) * CH, :] = piece


def pool_matrix():
    pixel = lax.broadcasted_iota(jnp.int32, (PIX, CELLS), 0)
    cell = lax.broadcasted_iota(jnp.int32, (PIX, CELLS), 1)
    square = ((pixel >> 6) << 4) + ((pixel & (SIDE - 1)) >> 1)
    return square == cell


def spread_matrix():
    cell = lax.broadcasted_iota(jnp.int32, (CELLS, PIX), 0)
    pixel = lax.broadcasted_iota(jnp.int32, (CELLS, PIX), 1)
    square = ((pixel >> 6) << 4) + ((pixel & (SIDE - 1)) >> 1)
    return (square == cell).astype(F32).astype(BF)


def prep_kernel(states_ref, filters_ref, act_ref, slope_ref, matrix_ref):
    total = filters_ref[:, 0:CH].astype(F32)
    for t in range(1, TAPS):
        total += filters_ref[:, t * CH : (t + 1) * CH].astype(F32)
    row = lax.broadcasted_iota(jnp.int32, (CH, CH), 0)
    col = lax.broadcasted_iota(jnp.int32, (CH, CH), 1)
    base = jnp.where(row == col, KEEP, 0.0) + STEP * total
    matrix = dot(base, base, EXACT)
    for j in range(XS):
        matrix_ref[j] = matrix
    for l in range(2):
        act = jnp.tanh(states_ref[l].astype(F32))
        act_ref[l] = act.astype(BF)
        slope_ref[l] = STEP * (1.0 - act * act)


def fine_kernel(above_ref, terminal_ref, guess_ref, slope_ref, filters_ref, top_ref, coarse_ref, stack_ref):
    last = lax.axis_index("layer") == XS * YS - 1
    top = jnp.where(last, terminal_ref[...].astype(F32), above_ref[...].astype(F32))
    top_ref[...] = top.astype(BF)
    write_stack(top.astype(BF), stack_ref)
    below = (KEEP * top + slope_ref[1] * dot(filters_ref[1], stack_ref[...])).astype(BF)
    write_stack(below, stack_ref)
    residual = KEEP * below.astype(F32) + slope_ref[0] * dot(filters_ref[0], stack_ref[...])
    residual -= guess_ref[...].astype(F32)
    high, low = split(residual)
    pool = jnp.where(pool_matrix(), 0.25, 0.0).astype(BF)
    coarse = (dot(high, pool) + dot(low, pool)).astype(BF)
    for j in range(XS):
        coarse_ref[j] = coarse


def group_kernel(matrix_ref, part_ref, reach_ref, group_ref, row_scr, reach_scr):
    m0, m1, m2, m3 = (matrix_ref[j] for j in range(XS))
    p01, p12, p23 = dot(m0, m1, EXACT), dot(m1, m2, EXACT), dot(m2, m3, EXACT)
    p012, p123, group = dot(p01, m2, EXACT), dot(p12, m3, EXACT), dot(p01, p23, EXACT)
    for j in range(YS):
        group_ref[j] = group
    row = lax.broadcasted_iota(jnp.int32, (CH, CH), 0)
    col = lax.broadcasted_iota(jnp.int32, (CH, CH), 1)
    one = jnp.where(row == col, 1.0, 0.0)
    nil = jnp.zeros((CH, CH), F32)
    table = (
        (one, m0, p01, p012),
        (nil, one, m1, p12),
        (nil, nil, one, m2),
        (nil, nil, nil, one),
        (nil, nil, nil, nil),
    )
    for s in range(5):
        for j in range(4):
            row_scr[s, :, j * CH : (j + 1) * CH] = table[s][j]
    for s, reach in enumerate((group, p123, p23, m3, one)):
        reach_scr[s] = reach
    x = lax.axis_index("layer") % XS
    for i, s in enumerate((0, x, x + 1)):
        high, low = split(row_scr[s])
        part_ref[i * CH : (i + 1) * CH, : XS * CH] = high
        part_ref[i * CH : (i + 1) * CH, XS * CH :] = low
    reach_ref[:CH] = reach_scr[x]
    reach_ref[CH:] = reach_scr[x + 1]


def local_kernel(part_ref, coarse_ref, value_ref, local_ref):
    coarse = coarse_ref[...].reshape(XS * CH, CELLS)
    part = dot(part_ref[:, : XS * CH], coarse) + dot(part_ref[:, XS * CH :], coarse)
    value = part[:CH].astype(BF)
    for j in range(YS):
        value_ref[j] = value
    local_ref[...] = part[CH:]


def reach_kernel(group_ref, reach_ref, far_ref):
    y = lax.axis_index("layer") // XS
    reach = reach_ref[...]
    nil = jnp.zeros_like(reach)
    for j in range(YS):
        ahead = j > y
        high, low = split(jnp.where(ahead, reach, nil))
        far_ref[:, j * CH : (j + 1) * CH] = high
        far_ref[:, (YS + j) * CH : (YS + j + 1) * CH] = low
        if j < YS - 1:
            reach = jnp.where(ahead, dot(reach, group_ref[j], EXACT), reach)


def correct_kernel(
    far_ref, value_ref, local_ref, top_ref, guess_ref, slope_ref, act_ref, filters_ref,
    adjoint_ref, keep_ref, send_ref, stack_ref, grad_scr,
):
    value = value_ref[...].reshape(YS * CH, CELLS)
    error = local_ref[...] + dot(far_ref[:, : YS * CH], value) + dot(far_ref[:, YS * CH :], value)
    high, low = split(error)
    spread = spread_matrix()
    wide = dot(high, spread) + dot(low, spread)
    adjoint_ref[0] = (guess_ref[...].astype(F32) + wide[:CH]).astype(BF)
    top = (top_ref[...].astype(F32) + wide[CH:]).astype(BF)
    nt = (((1,), (1,)), ((), ()))

    def gradient(l):
        grad = STEP * lax.dot_general(act_ref[l], stack_ref[...], nt, preferred_element_type=F32)
        grad_scr[:, :, l] = grad.reshape(ZS, 2, 8, TAPS * CH)

    write_stack(top, stack_ref)
    below = KEEP * top.astype(F32) + slope_ref[1] * dot(filters_ref[1], stack_ref[...])
    gradient(1)
    below = below.astype(BF)
    adjoint_ref[1] = below
    write_stack(below, stack_ref)
    gradient(0)
    core = lax.axis_index("dp") % 2
    keep_ref[...] = grad_scr[:, core]
    send_ref[...] = grad_scr[:, 1 - core].astype(BF)


def join_kernel(keep_ref, came_ref, sum_ref):
    sum_ref[...] = (keep_ref[...] + came_ref[...].astype(F32)).astype(BF)


def total_kernel(came_ref, grad_ref):
    total = came_ref[0].astype(F32)
    for z in range(1, ZS):
        total += came_ref[z].astype(F32)
    grad_ref[...] = total


def call(body, outs, scratch=(), flops=10**6, name=None):
    outs = [jax.ShapeDtypeStruct(s, d) for s, d in outs]
    single = len(outs) == 1
    return pl.pallas_call(
        body,
        out_shape=outs[0] if single else outs,
        scratch_shapes=[pltpu.VMEM(s, d) for s, d in scratch],
        name=name,
        compiler_params=pltpu.CompilerParams(vmem_limit_bytes=48 << 20),
        cost_estimate=pl.CostEstimate(flops=flops, bytes_accessed=1 << 20, transcendentals=0),
    )


STACK = ((TAPS * CH, PIX), BF)
prep = call(prep_kernel, [((2, CH, PIX), BF), ((2, CH, PIX), F32), ((XS, CH, CH), F32)])
fine = call(fine_kernel, [((CH, PIX), BF), ((XS, CH, CELLS), BF)], [STACK], 10**9)
group_of = call(
    group_kernel,
    [((3 * CH, 2 * XS * CH), BF), ((2 * CH, CH), F32), ((YS, CH, CH), F32)],
    [((5, CH, XS * CH), F32), ((5, CH, CH), F32)],
)
local_of = call(local_kernel, [((YS, CH, CELLS), BF), ((2 * CH, CELLS), F32)])
reach_of = call(reach_kernel, [((2 * CH, 2 * YS * CH), BF)])
correct = call(
    correct_kernel,
    [((2, CH, PIX), BF), ((ZS, 2, 8, TAPS * CH), F32), ((ZS, 2, 8, TAPS * CH), BF)],
    [STACK, ((ZS, 2, 2, 8, TAPS * CH), F32)],
    2 * 10**9,
)
join = call(join_kernel, [((ZS, 2, 8, TAPS * CH), BF)])
total_of = call(total_kernel, [((2, 8, TAPS * CH), F32)])


def per_device(states, filters, guess, terminal):
    states, guess, terminal = states[:, 0], guess[:, 0], terminal[0]
    x_groups = [[y * XS + x for x in range(XS)] for y in range(YS)]
    y_groups = [[y * XS + x for y in range(YS)] for x in range(XS)]
    z_groups = [[z * 2 + c for z in range(ZS)] for c in range(2)]

    def exchange(a, axis, groups):
        return lax.all_to_all(a, axis, 0, 0, axis_index_groups=groups)

    above = lax.ppermute(guess[0], "layer", [(i + 1, i) for i in range(XS * YS - 1)])
    act, slope, matrix = prep(states, filters[0])
    matrices = exchange(matrix, "layer", x_groups)
    top, coarse = fine(above, terminal, guess[0], slope, filters)
    coarses = exchange(coarse, "layer", x_groups)
    part, reach, group = group_of(matrices)
    groups = exchange(group, "layer", y_groups)
    value, local = local_of(part, coarses)
    values = exchange(value, "layer", y_groups)
    far = reach_of(groups, reach)
    adjoint, keep, send = correct(far, values, local, top, guess[0], slope, act, filters)
    came = lax.ppermute(send, "dp", [(i ^ 1, i) for i in range(2 * ZS)])
    shares = exchange(join(keep, came), "dp", z_groups)
    return adjoint[:, None], total_of(shares)


def solution(mesh):
    return jax.shard_map(
        per_device,
        mesh=mesh,
        in_specs=(
            P("layer", "dp", None, None),
            P("layer", None, None),
            P("layer", "dp", None, None),
            P("dp", None, None),
        ),
        out_specs=(P("layer", "dp", None, None), P("layer", "dp", None)),
        check_vma=False,
    )
```

```python
import functools

import jax
import jax.numpy as jnp
from jax import lax
from jax.experimental import pallas as pl
from jax.experimental.pallas import tpu as pltpu
from jax.sharding import PartitionSpec as P

STEP = 0.0625
KEEP = 1.0 - STEP
SIDE, PIX, CH, TAPS = 32, 1024, 128, 9
HALF = SIDE // 2
CELLS = HALF * HALF
XS, YS, ZS = 4, 8, 8
BF, F32 = jnp.bfloat16, jnp.float32
EXACT = lax.Precision.HIGHEST
VMEM = pl.BlockSpec(memory_space=pltpu.VMEM)


def dot(a, b, precision=None):
    return jnp.dot(a, b, preferred_element_type=F32, precision=precision)


def split(a):
    high = a.astype(BF)
    return high, (a - high.astype(F32)).astype(BF)


def write_stack(field, stack_ref):
    lane = lax.broadcasted_iota(jnp.int32, (1, PIX), 1)
    col = lane & (SIDE - 1)
    first, last = (col != 0).astype(BF), (col != SIDE - 1).astype(BF)
    top, bottom = (lane >= SIDE).astype(BF), (lane < PIX - SIDE).astype(BF)
    columns = (
        pltpu.roll(field, PIX - 1, 1) * last,
        field,
        pltpu.roll(field, 1, 1) * first,
    )
    for c, moved in enumerate(columns):
        rows = (
            pltpu.roll(moved, PIX - SIDE, 1) * bottom,
            moved,
            pltpu.roll(moved, SIDE, 1) * top,
        )
        for a, piece in enumerate(rows):
            t = 3 * a + c
            stack_ref[t * CH : (t + 1) * CH, :] = piece


def pool_matrix():
    pixel = lax.broadcasted_iota(jnp.int32, (PIX, CELLS), 0)
    cell = lax.broadcasted_iota(jnp.int32, (PIX, CELLS), 1)
    square = ((pixel >> 6) << 4) + ((pixel & (SIDE - 1)) >> 1)
    return square == cell


def spread_matrix():
    cell = lax.broadcasted_iota(jnp.int32, (CELLS, PIX), 0)
    pixel = lax.broadcasted_iota(jnp.int32, (CELLS, PIX), 1)
    square = ((pixel >> 6) << 4) + ((pixel & (SIDE - 1)) >> 1)
    return (square == cell).astype(F32).astype(BF)


def times(high, low, right):
    right_high, right_low = split(right)
    return dot(high, right_high) + dot(high, right_low) + dot(low, right_high)


def tanh_of(state):
    return jnp.tanh(state.astype(F32))


def slope_of(act):
    return STEP * (1.0 - act * act)


def prep_kernel(filters_ref, matrix_ref):
    total = filters_ref[0, :, 0:CH].astype(F32)
    for t in range(1, TAPS):
        total += filters_ref[0, :, t * CH : (t + 1) * CH].astype(F32)
    row = lax.broadcasted_iota(jnp.int32, (CH, CH), 0)
    col = lax.broadcasted_iota(jnp.int32, (CH, CH), 1)
    base = jnp.where(row == col, KEEP, 0.0) + STEP * total
    high, low = split(dot(base, base, EXACT))
    matrix_ref[:, :CH] = high
    matrix_ref[:, CH:] = low


def fine_kernel(
    above_ref, terminal_ref, guess_ref, states_ref, filters_ref, matrix_ref, top_ref, pack_ref, stack_ref
):
    last = lax.axis_index("layer") == XS * YS - 1
    top = jnp.where(last, terminal_ref[...].astype(F32), above_ref[...].astype(F32))
    top_ref[...] = top.astype(BF)
    write_stack(top.astype(BF), stack_ref)
    below = KEEP * top + slope_of(tanh_of(states_ref[1])) * dot(filters_ref[1], stack_ref[...])
    below = below.astype(BF)
    write_stack(below, stack_ref)
    moved = slope_of(tanh_of(states_ref[0])) * dot(filters_ref[0], stack_ref[...])
    residual = KEEP * below.astype(F32) + moved - guess_ref[...].astype(F32)
    high, low = split(residual)
    pool = jnp.where(pool_matrix(), 0.25, 0.0).astype(BF)
    coarse = (dot(high, pool) + dot(low, pool)).astype(BF)
    matrix = matrix_ref[...]
    for j in range(XS):
        pack_ref[j, :, :CELLS] = coarse
        pack_ref[j, :, CELLS:] = matrix


def group_kernel(packs_ref, pack_ref):
    value = packs_ref[XS - 1, :, :CELLS].astype(F32)
    highs = [packs_ref[j, :, CELLS : CELLS + CH] for j in range(XS)]
    lows = [packs_ref[j, :, CELLS + CH :] for j in range(XS)]
    for j in range(XS - 2, -1, -1):
        value = times(highs[j], lows[j], value) + packs_ref[j, :, :CELLS].astype(F32)
    full = [highs[j].astype(F32) + lows[j].astype(F32) for j in range(XS)]
    group = dot(dot(full[0], full[1], EXACT), dot(full[2], full[3], EXACT), EXACT)
    value = value.astype(BF)
    high, low = split(group)
    for j in range(YS):
        pack_ref[j, :, :CELLS] = value
        pack_ref[j, :, CELLS : CELLS + CH] = high
        pack_ref[j, :, CELLS + CH :] = low


def correct_kernel(
    groups_ref, packs_hbm, top_hbm, guess_hbm, states_hbm, filters_hbm,
    adjoint_ref, keep_ref, send_ref,
    packs_ref, top_ref, guess_ref, states_ref, filters_ref, stack_ref, grad_scr, sems,
):
    copies = [
        pltpu.make_async_copy(source, target, sems.at[i])
        for i, (source, target) in enumerate((
            (packs_hbm, packs_ref),
            (top_hbm, top_ref),
            (guess_hbm.at[0], guess_ref),
            (filters_hbm.at[1], filters_ref),
            (states_hbm, states_ref),
        ))
    ]
    for copy in copies:
        copy.start()
    layer = lax.axis_index("layer")
    x, y = layer % XS, layer // XS
    upper = jnp.zeros((CH, CELLS), F32)
    for j in range(YS - 1, 0, -1):
        moved = times(groups_ref[j, :, CELLS : CELLS + CH], groups_ref[j, :, CELLS + CH :], upper)
        upper = jnp.where(j > y, moved + groups_ref[j, :, :CELLS].astype(F32), upper)
    copies[0].wait()
    own = upper
    for j in range(XS - 1, -1, -1):
        moved = times(packs_ref[j, :, CELLS : CELLS + CH], packs_ref[j, :, CELLS + CH :], upper)
        moved += packs_ref[j, :, :CELLS].astype(F32)
        own = jnp.where(x == j, moved, own)
        upper = jnp.where(j > x, moved, upper)
    spread = spread_matrix()

    def widen(error):
        high, low = split(error)
        return dot(high, spread) + dot(low, spread)

    nt = (((1,), (1,)), ((), ()))

    def gradient(l, act):
        grad = STEP * lax.dot_general(act.astype(BF), stack_ref[...], nt, preferred_element_type=F32)
        grad_scr[:, :, l] = grad.reshape(ZS, 2, 8, TAPS * CH)

    copies[1].wait()
    top = (top_ref[...].astype(F32) + widen(upper)).astype(BF)
    write_stack(top, stack_ref)
    copies[2].wait()
    copies[3].wait()
    copies[4].wait()
    act = tanh_of(states_ref[1])
    below = (KEEP * top.astype(F32) + slope_of(act) * dot(filters_ref[...], stack_ref[...])).astype(BF)
    gradient(1, act)
    adjoint_ref[0] = (guess_ref[...].astype(F32) + widen(own)).astype(BF)
    adjoint_ref[1] = below
    write_stack(below, stack_ref)
    gradient(0, tanh_of(states_ref[0]))
    core = lax.axis_index("dp") % 2
    keep_ref[...] = grad_scr[:, core].reshape(ZS, 16, TAPS * CH)
    send_ref[...] = grad_scr[:, 1 - core].reshape(ZS, 16, TAPS * CH).astype(BF)


def join_kernel(keep_ref, came_ref, sum_ref):
    sum_ref[...] = (keep_ref[...] + came_ref[...].astype(F32)).astype(BF)


def total_kernel(came_ref, grad_ref):
    total = came_ref[0].astype(F32)
    for z in range(1, ZS):
        total += came_ref[z].astype(F32)
    grad_ref[...] = total.reshape(2, 8, TAPS * CH)


def call(body, outs, scratch=(), flops=10**6, vmem=6, in_specs=None):
    outs = [jax.ShapeDtypeStruct(s, d) for s, d in outs]
    extra = {} if in_specs is None else {"in_specs": in_specs}
    return pl.pallas_call(
        body,
        out_shape=outs[0] if len(outs) == 1 else outs,
        scratch_shapes=list(scratch),
        compiler_params=pltpu.CompilerParams(vmem_limit_bytes=vmem << 20),
        cost_estimate=pl.CostEstimate(flops=flops, bytes_accessed=1 << 20, transcendentals=0),
        **extra,
    )


WIDTH = CELLS + 2 * CH
FIELD = (CH, PIX)
STACK = pltpu.VMEM((TAPS * CH, PIX), BF)
SHARE = (ZS, 16, TAPS * CH)
ANY = pl.BlockSpec(memory_space=pl.ANY)
prep = call(prep_kernel, [((CH, 2 * CH), BF)])
fine = call(fine_kernel, [(FIELD, BF), ((XS, CH, WIDTH), BF)], [STACK], 10**9, 16)
group_of = call(group_kernel, [((YS, CH, WIDTH), BF)])
correct = call(
    correct_kernel,
    [((2,) + FIELD, BF), (SHARE, F32), (SHARE, BF)],
    [
        pltpu.VMEM((XS, CH, WIDTH), BF),
        pltpu.VMEM(FIELD, BF),
        pltpu.VMEM(FIELD, BF),
        pltpu.VMEM((2,) + FIELD, BF),
        pltpu.VMEM((CH, TAPS * CH), BF),
        STACK,
        pltpu.VMEM((ZS, 2, 2, 8, TAPS * CH), F32),
        pltpu.SemaphoreType.DMA((5,)),
    ],
    2 * 10**9,
    24,
    [VMEM] + [ANY] * 5,
)
join = call(join_kernel, [(SHARE, BF)])
total_of = call(total_kernel, [((2, 8, TAPS * CH), F32)])


def per_device(states, filters, guess, terminal):
    states, guess, terminal = states[:, 0], guess[:, 0], terminal[0]
    x_groups = [[y * XS + x for x in range(XS)] for y in range(YS)]
    y_groups = [[y * XS + x for y in range(YS)] for x in range(XS)]
    z_groups = [[z * 2 + c for z in range(ZS)] for c in range(2)]

    def exchange(a, axis, groups):
        return lax.all_to_all(a, axis, 0, 0, axis_index_groups=groups)

    above = lax.ppermute(guess[0], "layer", [(i + 1, i) for i in range(XS * YS - 1)])
    matrix = prep(filters)
    top, pack = fine(above, terminal, guess[0], states, filters, matrix)
    packs = exchange(pack, "layer", x_groups)
    groups = exchange(group_of(packs), "layer", y_groups)
    adjoint, keep, send = correct(groups, packs, top, guess, states, filters)
    came = lax.ppermute(send, "dp", [(i ^ 1, i) for i in range(2 * ZS)])
    shares = exchange(join(keep, came), "dp", z_groups)
    return adjoint[:, None], total_of(shares)


def solution(mesh):
    return jax.shard_map(
        per_device,
        mesh=mesh,
        in_specs=(
            P("layer", "dp", None, None),
            P("layer", None, None),
            P("layer", "dp", None, None),
            P("dp", None, None),
        ),
        out_specs=(P("layer", "dp", None, None), P("layer", "dp", None)),
        check_vma=False,
    )
```

```python
import functools

import jax
import jax.numpy as jnp
from jax import lax
from jax.experimental import pallas as pl
from jax.experimental.pallas import tpu as pltpu
from jax.sharding import PartitionSpec as P

STEP = 0.0625
KEEP = 1.0 - STEP
SIDE, PIX, CH, TAPS = 32, 1024, 128, 9
HALF = SIDE // 2
CELLS = HALF * HALF
XS, YS, ZS = 4, 8, 8
BF, F32 = jnp.bfloat16, jnp.float32
EXACT = lax.Precision.HIGHEST
VMEM = pl.BlockSpec(memory_space=pltpu.VMEM)


def dot(a, b, precision=None):
    return jnp.dot(a, b, preferred_element_type=F32, precision=precision)


def split(a):
    high = a.astype(BF)
    return high, (a - high.astype(F32)).astype(BF)


def write_stack(field, stack_ref):
    lane = lax.broadcasted_iota(jnp.int32, (1, PIX), 1)
    col = lane & (SIDE - 1)
    first, last = (col != 0).astype(BF), (col != SIDE - 1).astype(BF)
    top, bottom = (lane >= SIDE).astype(BF), (lane < PIX - SIDE).astype(BF)
    columns = (
        pltpu.roll(field, PIX - 1, 1) * last,
        field,
        pltpu.roll(field, 1, 1) * first,
    )
    for c, moved in enumerate(columns):
        rows = (
            pltpu.roll(moved, PIX - SIDE, 1) * bottom,
            moved,
            pltpu.roll(moved, SIDE, 1) * top,
        )
        for a, piece in enumerate(rows):
            t = 3 * a + c
            stack_ref[t * CH : (t + 1) * CH, :] = piece


def pool_matrix():
    pixel = lax.broadcasted_iota(jnp.int32, (PIX, CELLS), 0)
    cell = lax.broadcasted_iota(jnp.int32, (PIX, CELLS), 1)
    square = ((pixel >> 6) << 4) + ((pixel & (SIDE - 1)) >> 1)
    return square == cell


def spread_matrix():
    cell = lax.broadcasted_iota(jnp.int32, (CELLS, PIX), 0)
    pixel = lax.broadcasted_iota(jnp.int32, (CELLS, PIX), 1)
    square = ((pixel >> 6) << 4) + ((pixel & (SIDE - 1)) >> 1)
    return (square == cell).astype(F32).astype(BF)


def identity():
    row = lax.broadcasted_iota(jnp.int32, (CH, CH), 0)
    return jnp.where(row == lax.broadcasted_iota(jnp.int32, (CH, CH), 1), 1.0, 0.0)


def rounded(part):
    row = lax.broadcasted_iota(jnp.int32, (CH, CH), 0).astype(F32)
    col = lax.broadcasted_iota(jnp.int32, (CH, CH), 1).astype(F32)
    place = row * 0.7548776662 + col * 0.5698402910
    offset = place - jnp.floor(place) - 0.5
    return (part + part * offset * 0.00546875).astype(BF)


def times(scale, part, right):
    high, low = split(right)
    return scale * right + (dot(part, high) + dot(part, low))


def tanh_of(state):
    return jnp.tanh(state.astype(F32))


def slope_of(act):
    return STEP * (1.0 - act * act)


def prep_kernel(filters_ref, terminal_ref, matrix_ref, ending_ref):
    total = filters_ref[0, :, 0:CH].astype(F32)
    for t in range(1, TAPS):
        total += filters_ref[0, :, t * CH : (t + 1) * CH].astype(F32)
    total *= STEP
    matrix_ref[...] = rounded((2.0 * KEEP) * total + dot(total, total, EXACT))
    ending_ref[...] = terminal_ref[...]


def fine_kernel(
    above_ref, terminal_ref, guess_ref, states_hbm, filters_ref, matrix_ref,
    top_ref, pack_ref, states_ref, stack_ref, sem,
):
    fetch = pltpu.make_async_copy(states_hbm, states_ref, sem)
    fetch.start()
    last = lax.axis_index("layer") == XS * YS - 1
    top = jnp.where(last, terminal_ref[...].astype(F32), above_ref[...].astype(F32))
    top_ref[...] = top.astype(BF)
    write_stack(top.astype(BF), stack_ref)
    fetch.wait()
    below = KEEP * top + slope_of(tanh_of(states_ref[1])) * dot(filters_ref[1], stack_ref[...])
    below = below.astype(BF)
    write_stack(below, stack_ref)
    moved = slope_of(tanh_of(states_ref[0])) * dot(filters_ref[0], stack_ref[...])
    residual = KEEP * below.astype(F32) + moved - guess_ref[...].astype(F32)
    high, low = split(residual)
    pool = jnp.where(pool_matrix(), 0.25, 0.0).astype(BF)
    coarse = (dot(high, pool) + dot(low, pool)).astype(BF)
    matrix = matrix_ref[...]
    for j in range(XS):
        pack_ref[j, :, :CELLS] = coarse
        pack_ref[j, :, CELLS:] = matrix


def group_kernel(packs_ref, pack_ref):
    parts = [packs_ref[j, :, CELLS:] for j in range(XS)]
    value = packs_ref[XS - 1, :, :CELLS].astype(F32)
    for j in range(XS - 2, -1, -1):
        value = times(KEEP**2, parts[j], value) + packs_ref[j, :, :CELLS].astype(F32)
    one = identity()
    full = [KEEP**2 * one + part.astype(F32) for part in parts]
    group = dot(dot(full[0], full[1], EXACT), dot(full[2], full[3], EXACT), EXACT)
    value = value.astype(BF)
    part = rounded(group - KEEP**8 * one)
    for j in range(YS):
        pack_ref[j, :, :CELLS] = value
        pack_ref[j, :, CELLS:] = part


def correct_kernel(
    groups_ref, packs_hbm, top_hbm, guess_hbm, states_hbm, filters_hbm,
    adjoint_ref, keep_ref, send_ref,
    packs_ref, top_ref, guess_ref, states_ref, filters_ref, stack_ref, grad_scr, sems,
):
    copies = [
        pltpu.make_async_copy(source, target, sems.at[i])
        for i, (source, target) in enumerate((
            (packs_hbm, packs_ref),
            (top_hbm, top_ref),
            (guess_hbm.at[0], guess_ref),
            (filters_hbm.at[1], filters_ref),
            (states_hbm, states_ref),
        ))
    ]
    for copy in copies:
        copy.start()
    layer = lax.axis_index("layer")
    x, y = layer % XS, layer // XS
    upper = jnp.zeros((CH, CELLS), F32)
    for j in range(YS - 1, 0, -1):
        moved = times(KEEP**8, groups_ref[j, :, CELLS:], upper)
        upper = jnp.where(j > y, moved + groups_ref[j, :, :CELLS].astype(F32), upper)
    copies[0].wait()
    own = upper
    for j in range(XS - 1, -1, -1):
        moved = times(KEEP**2, packs_ref[j, :, CELLS:], upper)
        moved += packs_ref[j, :, :CELLS].astype(F32)
        own = jnp.where(x == j, moved, own)
        upper = jnp.where(j > x, moved, upper)
    spread = spread_matrix()

    def widen(error):
        high, low = split(error)
        return dot(high, spread) + dot(low, spread)

    nt = (((1,), (1,)), ((), ()))

    def gradient(l, act):
        grad = STEP * lax.dot_general(act.astype(BF), stack_ref[...], nt, preferred_element_type=F32)
        grad_scr[:, :, l] = grad.reshape(ZS, 2, 8, TAPS * CH)

    copies[1].wait()
    top = (top_ref[...].astype(F32) + widen(upper)).astype(BF)
    write_stack(top, stack_ref)
    copies[2].wait()
    copies[3].wait()
    copies[4].wait()
    act = tanh_of(states_ref[1])
    below = (KEEP * top.astype(F32) + slope_of(act) * dot(filters_ref[...], stack_ref[...])).astype(BF)
    gradient(1, act)
    adjoint_ref[0] = (guess_ref[...].astype(F32) + widen(own)).astype(BF)
    adjoint_ref[1] = below
    write_stack(below, stack_ref)
    gradient(0, tanh_of(states_ref[0]))
    core = lax.axis_index("dp") % 2
    keep_ref[...] = grad_scr[:, core].reshape(ZS, 16, TAPS * CH)
    send_ref[...] = grad_scr[:, 1 - core].reshape(ZS, 16, TAPS * CH).astype(BF)


def join_kernel(keep_ref, came_ref, sum_ref):
    sum_ref[...] = (keep_ref[...] + came_ref[...].astype(F32)).astype(BF)


def total_kernel(came_ref, grad_ref):
    total = came_ref[0].astype(F32)
    for z in range(1, ZS):
        total += came_ref[z].astype(F32)
    grad_ref[...] = total.reshape(2, 8, TAPS * CH)


def call(body, outs, scratch=(), flops=10**6, vmem=6, in_specs=None):
    outs = [jax.ShapeDtypeStruct(s, d) for s, d in outs]
    extra = {} if in_specs is None else {"in_specs": in_specs}
    return pl.pallas_call(
        body,
        out_shape=outs[0] if len(outs) == 1 else outs,
        scratch_shapes=list(scratch),
        compiler_params=pltpu.CompilerParams(vmem_limit_bytes=vmem << 20),
        cost_estimate=pl.CostEstimate(flops=flops, bytes_accessed=1 << 20, transcendentals=0),
        **extra,
    )


WIDTH = CELLS + CH
FIELD = (CH, PIX)
STACK = pltpu.VMEM((TAPS * CH, PIX), BF)
SHARE = (ZS, 16, TAPS * CH)
ANY = pl.BlockSpec(memory_space=pl.ANY)
prep = call(prep_kernel, [((CH, CH), BF), (FIELD, BF)])
fine = call(
    fine_kernel,
    [(FIELD, BF), ((XS, CH, WIDTH), BF)],
    [pltpu.VMEM((2,) + FIELD, BF), STACK, pltpu.SemaphoreType.DMA(())],
    10**9,
    16,
    [VMEM] * 3 + [ANY] + [VMEM] * 2,
)
group_of = call(group_kernel, [((YS, CH, WIDTH), BF)])
correct = call(
    correct_kernel,
    [((2,) + FIELD, BF), (SHARE, F32), (SHARE, BF)],
    [
        pltpu.VMEM((XS, CH, WIDTH), BF),
        pltpu.VMEM(FIELD, BF),
        pltpu.VMEM(FIELD, BF),
        pltpu.VMEM((2,) + FIELD, BF),
        pltpu.VMEM((CH, TAPS * CH), BF),
        STACK,
        pltpu.VMEM((ZS, 2, 2, 8, TAPS * CH), F32),
        pltpu.SemaphoreType.DMA((5,)),
    ],
    2 * 10**9,
    24,
    [VMEM] + [ANY] * 5,
)
join = call(join_kernel, [(SHARE, BF)])
total_of = call(total_kernel, [((2, 8, TAPS * CH), F32)])


def per_device(states, filters, guess, terminal):
    states, guess, terminal = states[:, 0], guess[:, 0], terminal[0]
    x_groups = [[y * XS + x for x in range(XS)] for y in range(YS)]
    y_groups = [[y * XS + x for y in range(YS)] for x in range(XS)]
    z_groups = [[z * 2 + c for z in range(ZS)] for c in range(2)]

    def exchange(a, axis, groups):
        return lax.all_to_all(a, axis, 0, 0, axis_index_groups=groups)

    above = lax.ppermute(guess[0], "layer", [(i + 1, i) for i in range(XS * YS - 1)])
    matrix, ending = prep(filters, terminal)
    top, pack = fine(above, ending, guess[0], states, filters, matrix)
    packs = exchange(pack, "layer", x_groups)
    groups = exchange(group_of(packs), "layer", y_groups)
    adjoint, keep, send = correct(groups, packs, top, guess, states, filters)
    came = lax.ppermute(send, "dp", [(i ^ 1, i) for i in range(2 * ZS)])
    shares = exchange(join(keep, came), "dp", z_groups)
    return adjoint[:, None], total_of(shares)


def solution(mesh):
    return jax.shard_map(
        per_device,
        mesh=mesh,
        in_specs=(
            P("layer", "dp", None, None),
            P("layer", None, None),
            P("layer", "dp", None, None),
            P("dp", None, None),
        ),
        out_specs=(P("layer", "dp", None, None), P("layer", "dp", None)),
        check_vma=False,
    )
```

```python
import functools

import jax
import jax.numpy as jnp
from jax import lax
from jax.experimental import pallas as pl
from jax.experimental.pallas import tpu as pltpu
from jax.sharding import PartitionSpec as P

STEP = 0.0625
KEEP = 1.0 - STEP
SIDE, PIX, CH, TAPS = 32, 1024, 128, 9
HALF = SIDE // 2
CELLS = HALF * HALF
XS, YS, ZS = 4, 8, 8
BF, F32 = jnp.bfloat16, jnp.float32
EXACT = lax.Precision.HIGHEST
VMEM = pl.BlockSpec(memory_space=pltpu.VMEM)


def dot(a, b, precision=None):
    return jnp.dot(a, b, preferred_element_type=F32, precision=precision)


def split(a):
    high = a.astype(BF)
    return high, (a - high.astype(F32)).astype(BF)


def write_stack(field, stack_ref):
    lane = lax.broadcasted_iota(jnp.int32, (1, PIX), 1)
    col = lane & (SIDE - 1)
    first, last = (col != 0).astype(BF), (col != SIDE - 1).astype(BF)
    top, bottom = (lane >= SIDE).astype(BF), (lane < PIX - SIDE).astype(BF)
    columns = (
        pltpu.roll(field, PIX - 1, 1) * last,
        field,
        pltpu.roll(field, 1, 1) * first,
    )
    for c, moved in enumerate(columns):
        rows = (
            pltpu.roll(moved, PIX - SIDE, 1) * bottom,
            moved,
            pltpu.roll(moved, SIDE, 1) * top,
        )
        for a, piece in enumerate(rows):
            t = 3 * a + c
            stack_ref[t * CH : (t + 1) * CH, :] = piece


def pool_matrix():
    pixel = lax.broadcasted_iota(jnp.int32, (PIX, CELLS), 0)
    cell = lax.broadcasted_iota(jnp.int32, (PIX, CELLS), 1)
    square = ((pixel >> 6) << 4) + ((pixel & (SIDE - 1)) >> 1)
    return square == cell


def spread_matrix():
    cell = lax.broadcasted_iota(jnp.int32, (CELLS, PIX), 0)
    pixel = lax.broadcasted_iota(jnp.int32, (CELLS, PIX), 1)
    square = ((pixel >> 6) << 4) + ((pixel & (SIDE - 1)) >> 1)
    return (square == cell).astype(F32).astype(BF)


def identity():
    row = lax.broadcasted_iota(jnp.int32, (CH, CH), 0)
    return jnp.where(row == lax.broadcasted_iota(jnp.int32, (CH, CH), 1), 1.0, 0.0)


def rounded(part):
    row = lax.broadcasted_iota(jnp.int32, (CH, CH), 0).astype(F32)
    col = lax.broadcasted_iota(jnp.int32, (CH, CH), 1).astype(F32)
    place = row * 0.7548776662 + col * 0.5698402910
    offset = place - jnp.floor(place) - 0.5
    return (part + part * offset * 0.00546875).astype(BF)


def times(left, right):
    left_high, left_low = split(left)
    right_high, right_low = split(right)
    return dot(left_high, right_high) + dot(left_high, right_low) + dot(left_low, right_high)


def times_part(part, right):
    high, low = split(right)
    return dot(part, high) + dot(part, low)


def tanh_of(state):
    return jnp.tanh(state.astype(F32))


def slope_of(act):
    return STEP * (1.0 - act * act)


def prep_kernel(filters_ref, terminal_ref, states_ref, matrix_ref, ending_ref, kept_ref, lent_ref):
    total = filters_ref[0, :, 0:CH].astype(F32)
    for t in range(1, TAPS):
        total += filters_ref[0, :, t * CH : (t + 1) * CH].astype(F32)
    total *= STEP
    matrix_ref[...] = rounded((2.0 * KEEP) * total + dot(total, total, EXACT))
    ending_ref[...] = terminal_ref[...]
    kept_ref[...] = states_ref[...]
    lent_ref[...] = states_ref[lax.axis_index("dp") % 2]


def fine_kernel(
    above_ref, terminal_ref, guess_ref, states_ref, filters_ref, matrix_ref, top_ref, pack_ref, stack_ref
):
    last = lax.axis_index("layer") == XS * YS - 1
    top = jnp.where(last, terminal_ref[...].astype(F32), above_ref[...].astype(F32))
    top_ref[...] = top.astype(BF)
    write_stack(top.astype(BF), stack_ref)
    below = KEEP * top + slope_of(tanh_of(states_ref[1])) * dot(filters_ref[1], stack_ref[...])
    below = below.astype(BF)
    write_stack(below, stack_ref)
    moved = slope_of(tanh_of(states_ref[0])) * dot(filters_ref[0], stack_ref[...])
    residual = KEEP * below.astype(F32) + moved - guess_ref[...].astype(F32)
    high, low = split(residual)
    pool = jnp.where(pool_matrix(), 0.25, 0.0).astype(BF)
    coarse = (dot(high, pool) + dot(low, pool)).astype(BF)
    matrix = matrix_ref[...]
    for j in range(XS):
        pack_ref[j, :, :CELLS] = coarse
        pack_ref[j, :, CELLS:] = matrix


def group_kernel(packs_ref, pack_ref):
    scale = KEEP**2
    coarse = [packs_ref[j, :, :CELLS] for j in range(XS)]
    part = [packs_ref[j, :, CELLS:] for j in range(XS)]
    near, far = (
        coarse[j].astype(F32) + scale * coarse[j + 1].astype(F32) + dot(part[j], coarse[j + 1]) for j in (0, 2)
    )
    left, right = (
        scale * (part[j].astype(F32) + part[j + 1].astype(F32)) + dot(part[j], part[j + 1]) for j in (0, 2)
    )
    value = (near + scale**2 * far + times(left, far)).astype(BF)
    group = rounded(scale**2 * (left + right) + times(left, right))
    for j in range(YS):
        pack_ref[j, :, :CELLS] = value
        pack_ref[j, :, CELLS:] = group


def upper_error(groups_ref, y):
    scale = KEEP**8
    pairs = []
    for a in range(0, YS, 2):
        on = [(a + i > y).astype(F32) for i in range(2)]
        hold = [jnp.where(a + i > y, scale, 1.0) for i in range(2)]
        values = [groups_ref[a + i, :, :CELLS] for i in range(2)]
        parts = [groups_ref[a + i, :, CELLS:] for i in range(2)]
        mixed = hold[0] * values[1].astype(F32) + on[0] * dot(parts[0], values[1])
        field = on[0] * values[0].astype(F32) + on[1] * mixed
        crossed = (hold[0] * on[1]) * parts[1].astype(F32) + (hold[1] * on[0]) * parts[0].astype(F32)
        crossed += (on[0] * on[1]) * dot(parts[0], parts[1])
        pairs.append((field, hold[0] * hold[1], crossed))

    def joined(low, high):
        return low[0] + low[1] * high[0] + times(low[2], high[0])

    near, far = joined(pairs[0], pairs[1]), joined(pairs[2], pairs[3])
    hold = pairs[0][1] * pairs[1][1]
    crossed = pairs[0][1] * pairs[1][2] + pairs[1][1] * pairs[0][2] + times(pairs[0][2], pairs[1][2])
    return near + hold * far + times(crossed, far)


def local_maps(packs_ref):
    scale = KEEP**2
    coarse = [packs_ref[j, :, :CELLS] for j in range(XS)]
    part = [packs_ref[j, :, CELLS:] for j in range(XS)]
    field, hold, crossed = coarse[3].astype(F32), scale, part[3].astype(F32)
    maps = [(field, hold, crossed)]
    for j in (2, 1, 0):
        field = coarse[j].astype(F32) + scale * field + times_part(part[j], field)
        crossed = scale * crossed + hold * part[j].astype(F32) + times_part(part[j], crossed)
        hold *= scale
        maps.append((field, hold, crossed))
    return maps[::-1]


def correct_kernel(
    groups_ref, packs_hbm, top_hbm, guess_hbm, states_hbm, filters_hbm,
    adjoint_ref, own_ref, lent_ref, act_ref,
    packs_ref, top_ref, guess_ref, states_ref, filters_ref, stack_ref, next_scr, act_scr, sems,
):
    copies = [
        pltpu.make_async_copy(source, target, sems.at[i])
        for i, (source, target) in enumerate((
            (packs_hbm, packs_ref),
            (top_hbm, top_ref),
            (states_hbm, states_ref),
            (guess_hbm.at[0], guess_ref),
            (filters_hbm.at[1], filters_ref),
        ))
    ]
    for copy in copies:
        copy.start()
    layer = lax.axis_index("layer")
    core = lax.axis_index("dp") % 2
    x, y = layer % XS, layer // XS
    copies[0].wait()
    maps = local_maps(packs_ref)
    nil = (jnp.zeros((CH, CELLS), F32), 1.0, jnp.zeros((CH, CH), F32))
    own_map, upper_map = maps[XS - 1], nil
    for j in range(XS - 2, -1, -1):
        own_map = tuple(jnp.where(x == j, a, b) for a, b in zip(maps[j], own_map))
        upper_map = tuple(jnp.where(x == j, a, b) for a, b in zip(maps[j + 1], upper_map))
    far = upper_error(groups_ref, y)
    spread = spread_matrix()

    def widened(local):
        high, low = split(local[0] + local[1] * far + times(local[2], far))
        return dot(high, spread) + dot(low, spread)

    copies[1].wait()
    top = (top_ref[...].astype(F32) + widened(upper_map)).astype(BF)
    write_stack(top, stack_ref)
    copies[2].wait()
    copies[3].wait()
    copies[4].wait()
    act = tanh_of(states_ref[1])
    below = KEEP * top.astype(F32) + slope_of(act) * dot(filters_ref[...], stack_ref[...])
    below = below.astype(BF)
    next_scr[1] = top
    next_scr[0] = below
    act_scr[1] = act.astype(BF)
    act_scr[0] = tanh_of(states_ref[0]).astype(BF)
    adjoint_ref[0] = (guess_ref[...].astype(F32) + widened(own_map)).astype(BF)
    adjoint_ref[1] = below
    lent_ref[...] = next_scr[core]
    own_ref[...] = next_scr[1 - core]
    act_ref[...] = act_scr[1 - core]


def gradient_of(act, field, stack_ref):
    write_stack(field, stack_ref)
    contract = (((1,), (1,)), ((), ()))
    return STEP * lax.dot_general(act, stack_ref[...], contract, preferred_element_type=F32)


def own_kernel(adjoint_ref, own_ref, act_ref, other_ref, out_hbm, grad_ref, other_act_ref, stack_ref, sem):
    copy = pltpu.make_async_copy(adjoint_ref, out_hbm, sem)
    copy.start()
    other_act_ref[...] = tanh_of(other_ref[...]).astype(BF)
    grad_ref[...] = gradient_of(act_ref[...], own_ref[...], stack_ref)
    copy.wait()


def other_kernel(came_ref, other_act_ref, grad_ref, share_ref, stack_ref):
    grad = grad_ref[...] + gradient_of(other_act_ref[...], came_ref[...], stack_ref)
    share_ref[...] = grad.reshape(2 * ZS, 8, TAPS * CH).astype(BF)


def total_kernel(came_ref, grad_ref):
    for l in range(2):
        total = came_ref[1 - l].astype(F32)
        for z in range(1, ZS):
            total += came_ref[2 * z + 1 - l].astype(F32)
        grad_ref[l] = total


def call(body, outs, scratch=(), flops=10**6, vmem=6, in_specs=None, out_specs=None):
    outs = [jax.ShapeDtypeStruct(s, d) for s, d in outs]
    extra = {} if in_specs is None else {"in_specs": in_specs}
    if out_specs is not None:
        extra["out_specs"] = out_specs
    return pl.pallas_call(
        body,
        out_shape=outs[0] if len(outs) == 1 else outs,
        scratch_shapes=list(scratch),
        compiler_params=pltpu.CompilerParams(vmem_limit_bytes=vmem << 20),
        cost_estimate=pl.CostEstimate(flops=flops, bytes_accessed=1 << 20, transcendentals=0),
        **extra,
    )


WIDTH = CELLS + CH
FIELD = (CH, PIX)
STACK = pltpu.VMEM((TAPS * CH, PIX), BF)
ANY = pl.BlockSpec(memory_space=pl.ANY)
prep = call(prep_kernel, [((CH, CH), BF), (FIELD, BF), ((2,) + FIELD, BF), (FIELD, BF)])
fine = call(fine_kernel, [(FIELD, BF), ((XS, CH, WIDTH), BF)], [STACK], 10**9, 16)
group_of = call(group_kernel, [((YS, CH, WIDTH), BF)])
correct = call(
    correct_kernel,
    [((2,) + FIELD, BF), (FIELD, BF), (FIELD, BF), (FIELD, BF)],
    [
        pltpu.VMEM((XS, CH, WIDTH), BF),
        pltpu.VMEM(FIELD, BF),
        pltpu.VMEM(FIELD, BF),
        pltpu.VMEM((2,) + FIELD, BF),
        pltpu.VMEM((CH, TAPS * CH), BF),
        STACK,
        pltpu.VMEM((2,) + FIELD, BF),
        pltpu.VMEM((2,) + FIELD, BF),
        pltpu.SemaphoreType.DMA((5,)),
    ],
    10**9,
    20,
    [VMEM] + [ANY] * 5,
)
own_part = call(
    own_kernel,
    [((2,) + FIELD, BF), ((CH, TAPS * CH), F32), (FIELD, BF)],
    [STACK, pltpu.SemaphoreType.DMA(())],
    10**9,
    12,
    [VMEM] * 4,
    [ANY, VMEM, VMEM],
)
other_part = call(other_kernel, [((2 * ZS, 8, TAPS * CH), BF)], [STACK], 10**9, 12)
total_of = call(total_kernel, [((2, 8, TAPS * CH), F32)])


def per_device(states, filters, guess, terminal):
    states, guess, terminal = states[:, 0], guess[:, 0], terminal[0]
    x_groups = [[y * XS + x for x in range(XS)] for y in range(YS)]
    y_groups = [[y * XS + x for y in range(YS)] for x in range(XS)]

    def exchange(a, axis, groups):
        return lax.all_to_all(a, axis, 0, 0, axis_index_groups=groups)

    above = lax.ppermute(guess[0], "layer", [(i + 1, i) for i in range(XS * YS - 1)])
    matrix, ending, kept, lent = prep(filters, terminal, states)
    swap = [(i ^ 1, i) for i in range(2 * ZS)]
    other = lax.ppermute(lent, "dp", swap)
    above, other = lax.optimization_barrier((above, other))
    top, pack = fine(above, ending, guess[0], kept, filters, matrix)
    packs = exchange(pack, "layer", x_groups)
    groups = exchange(group_of(packs), "layer", y_groups)
    fresh, own, lent, act = correct(groups, packs, top, guess, states, filters)
    came = lax.ppermute(lent, "dp", swap)
    adjoint, grad, other_act = own_part(fresh, own, act, other)
    shares = lax.all_to_all(other_part(came, other_act, grad), "dp", 0, 0)
    return adjoint[:, None], total_of(shares)


def solution(mesh):
    return jax.shard_map(
        per_device,
        mesh=mesh,
        in_specs=(
            P("layer", "dp", None, None),
            P("layer", None, None),
            P("layer", "dp", None, None),
            P("dp", None, None),
        ),
        out_specs=(P("layer", "dp", None, None), P("layer", "dp", None)),
        check_vma=False,
    )
```

```python
import functools

import jax
import jax.numpy as jnp
from jax import lax
from jax.experimental import pallas as pl
from jax.experimental.pallas import tpu as pltpu
from jax.sharding import PartitionSpec as P

STEP = 0.0625
KEEP = 1.0 - STEP
SIDE, PIX, CH, TAPS = 32, 1024, 128, 9
HALF = SIDE // 2
CELLS = HALF * HALF
GROUP, GROUPS, ZS = 8, 4, 8
BF, F32 = jnp.bfloat16, jnp.float32
EXACT = lax.Precision.HIGHEST
VMEM = pl.BlockSpec(memory_space=pltpu.VMEM)


def dot(a, b, precision=None):
    return jnp.dot(a, b, preferred_element_type=F32, precision=precision)


def split(a):
    high = a.astype(BF)
    return high, (a - high.astype(F32)).astype(BF)


def write_stack(field, stack_ref):
    lane = lax.broadcasted_iota(jnp.int32, (1, PIX), 1)
    col = lane & (SIDE - 1)
    first, last = (col != 0).astype(BF), (col != SIDE - 1).astype(BF)
    top, bottom = (lane >= SIDE).astype(BF), (lane < PIX - SIDE).astype(BF)
    columns = (
        pltpu.roll(field, PIX - 1, 1) * last,
        field,
        pltpu.roll(field, 1, 1) * first,
    )
    for c, moved in enumerate(columns):
        rows = (
            pltpu.roll(moved, PIX - SIDE, 1) * bottom,
            moved,
            pltpu.roll(moved, SIDE, 1) * top,
        )
        for a, piece in enumerate(rows):
            t = 3 * a + c
            stack_ref[t * CH : (t + 1) * CH, :] = piece


def pool_matrix():
    pixel = lax.broadcasted_iota(jnp.int32, (PIX, CELLS), 0)
    cell = lax.broadcasted_iota(jnp.int32, (PIX, CELLS), 1)
    square = ((pixel >> 6) << 4) + ((pixel & (SIDE - 1)) >> 1)
    return square == cell


def spread_matrix():
    cell = lax.broadcasted_iota(jnp.int32, (CELLS, PIX), 0)
    pixel = lax.broadcasted_iota(jnp.int32, (CELLS, PIX), 1)
    square = ((pixel >> 6) << 4) + ((pixel & (SIDE - 1)) >> 1)
    return (square == cell).astype(F32).astype(BF)


def identity():
    row = lax.broadcasted_iota(jnp.int32, (CH, CH), 0)
    return jnp.where(row == lax.broadcasted_iota(jnp.int32, (CH, CH), 1), 1.0, 0.0)


def rounded(part):
    row = lax.broadcasted_iota(jnp.int32, (CH, CH), 0).astype(F32)
    col = lax.broadcasted_iota(jnp.int32, (CH, CH), 1).astype(F32)
    place = row * 0.7548776662 + col * 0.5698402910
    offset = place - jnp.floor(place) - 0.5
    return (part + part * offset * 0.00546875).astype(BF)


def times(left, right):
    left_high, left_low = split(left)
    right_high, right_low = split(right)
    return dot(left_high, right_high) + dot(left_high, right_low) + dot(left_low, right_high)


def times_part(part, right):
    high, low = split(right)
    return dot(part, high) + dot(part, low)


def tanh_of(state):
    return jnp.tanh(state.astype(F32))


def slope_of(act):
    return STEP * (1.0 - act * act)


def prep_kernel(filters_ref, terminal_ref, states_ref, matrix_ref, ending_ref, kept_ref, lent_ref):
    total = filters_ref[0, :, 0:CH].astype(F32)
    for t in range(1, TAPS):
        total += filters_ref[0, :, t * CH : (t + 1) * CH].astype(F32)
    total *= STEP
    matrix_ref[...] = rounded((2.0 * KEEP) * total + dot(total, total, EXACT))
    ending_ref[...] = terminal_ref[...]
    kept_ref[...] = states_ref[...]
    lent_ref[...] = states_ref[lax.axis_index("dp") % 2]


def fine_kernel(
    above_ref, terminal_ref, guess_ref, states_ref, filters_ref, matrix_ref, top_ref, pack_ref, stack_ref
):
    last = lax.axis_index("layer") == GROUP * GROUPS - 1
    top = jnp.where(last, terminal_ref[...].astype(F32), above_ref[...].astype(F32))
    top_ref[...] = top.astype(BF)
    write_stack(top.astype(BF), stack_ref)
    below = KEEP * top + slope_of(tanh_of(states_ref[1])) * dot(filters_ref[1], stack_ref[...])
    below = below.astype(BF)
    write_stack(below, stack_ref)
    moved = slope_of(tanh_of(states_ref[0])) * dot(filters_ref[0], stack_ref[...])
    residual = KEEP * below.astype(F32) + moved - guess_ref[...].astype(F32)
    high, low = split(residual)
    pool = jnp.where(pool_matrix(), 0.25, 0.0).astype(BF)
    coarse = (dot(high, pool) + dot(low, pool)).astype(BF)
    matrix = matrix_ref[...]
    for j in range(GROUP):
        pack_ref[j, :, :CELLS] = coarse
        pack_ref[j, :, CELLS:] = matrix


def paired(scale, fields, parts):
    near, far, left, right = fields[::2], fields[1::2], parts[::2], parts[1::2]
    joint = [a + scale * b + times(part, b) for a, b, part in zip(near, far, left)]
    mixed = [scale * (a + b) + times(a, b) for a, b in zip(left, right)]
    return scale * scale, joint, mixed


def group_kernel(packs_ref, pack_ref):
    scale = KEEP**2
    coarse = [packs_ref[j, :, :CELLS] for j in range(GROUP)]
    part = [packs_ref[j, :, CELLS:] for j in range(GROUP)]
    fields, parts = [], []
    for j in range(0, GROUP, 2):
        fields.append(coarse[j].astype(F32) + scale * coarse[j + 1].astype(F32) + dot(part[j], coarse[j + 1]))
        parts.append(scale * (part[j].astype(F32) + part[j + 1].astype(F32)) + dot(part[j], part[j + 1]))
    scale *= scale
    while len(fields) > 1:
        scale, fields, parts = paired(scale, fields, parts)
    value, group = fields[0].astype(BF), rounded(parts[0])
    for j in range(GROUPS):
        pack_ref[j, :, :CELLS] = value
        pack_ref[j, :, CELLS:] = group


def applied(local, error):
    return local[0] + local[1] * error + times(local[2], error)


def upper_error(groups_ref, at):
    scale = KEEP ** (2 * GROUP)
    pairs = []
    for a in range(0, GROUPS, 2):
        on = [(a + i > at).astype(F32) for i in range(2)]
        hold = [jnp.where(a + i > at, scale, 1.0) for i in range(2)]
        values = [groups_ref[a + i, :, :CELLS] for i in range(2)]
        parts = [groups_ref[a + i, :, CELLS:] for i in range(2)]
        mixed = hold[0] * values[1].astype(F32) + on[0] * dot(parts[0], values[1])
        field = on[0] * values[0].astype(F32) + on[1] * mixed
        crossed = (hold[0] * on[1]) * parts[1].astype(F32) + (hold[1] * on[0]) * parts[0].astype(F32)
        crossed += (on[0] * on[1]) * dot(parts[0], parts[1])
        pairs.append((field, hold[0] * hold[1], crossed))
    return applied(pairs[0], pairs[1][0])


def suffix_maps(packs_ref, first, last):
    scale = KEEP**2
    coarse = {j: packs_ref[j, :, :CELLS] for j in range(first, last + 1)}
    part = {j: packs_ref[j, :, CELLS:] for j in range(first, last + 1)}
    field, hold, crossed = coarse[last].astype(F32), scale, part[last].astype(F32)
    maps = {last: (field, hold, crossed)}
    for j in range(last - 1, first - 1, -1):
        field = coarse[j].astype(F32) + scale * field + times_part(part[j], field)
        crossed = scale * crossed + hold * part[j].astype(F32) + times_part(part[j], crossed)
        hold *= scale
        maps[j] = (field, hold, crossed)
    return maps


def picked(maps, default, at):
    for j, local in maps.items():
        default = tuple(jnp.where(at == j, a, b) for a, b in zip(local, default))
    return default


def correct_kernel(
    groups_ref, packs_hbm, top_hbm, guess_hbm, states_hbm, filters_hbm,
    adjoint_ref, own_ref, lent_ref, act_ref,
    packs_ref, top_ref, guess_ref, states_ref, filters_ref, stack_ref, next_scr, act_scr, sems,
):
    copies = [
        pltpu.make_async_copy(source, target, sems.at[i])
        for i, (source, target) in enumerate((
            (packs_hbm, packs_ref),
            (top_hbm, top_ref),
            (states_hbm, states_ref),
            (guess_hbm.at[0], guess_ref),
            (filters_hbm.at[1], filters_ref),
        ))
    ]
    for copy in copies:
        copy.start()
    layer = lax.axis_index("layer")
    core = lax.axis_index("dp") % 2
    place, at = layer % GROUP, layer // GROUP
    copies[0].wait()
    half = GROUP // 2
    low, high = suffix_maps(packs_ref, 0, half - 1), suffix_maps(packs_ref, half, GROUP - 1)
    nil = (jnp.zeros((CH, CELLS), F32), 1.0, jnp.zeros((CH, CH), F32))
    low_own = picked(low, nil, place)
    low_upper = picked({j - 1: low[j] for j in range(1, half)}, nil, place)
    high_own = picked({j: high[j] for j in range(half + 1, GROUP)}, high[half], place)
    high_upper = picked({j - 1: high[j] for j in range(half + 1, GROUP)}, high[half], place)
    high_upper = picked({GROUP - 1: nil}, high_upper, place)
    far = upper_error(groups_ref, at)
    spread = spread_matrix()

    def widened(near, beyond):
        high_part, low_part = split(applied(near, applied(beyond, far)))
        return dot(high_part, spread) + dot(low_part, spread)

    copies[1].wait()
    top = (top_ref[...].astype(F32) + widened(low_upper, high_upper)).astype(BF)
    write_stack(top, stack_ref)
    copies[2].wait()
    copies[3].wait()
    copies[4].wait()
    act = tanh_of(states_ref[1])
    below = KEEP * top.astype(F32) + slope_of(act) * dot(filters_ref[...], stack_ref[...])
    below = below.astype(BF)
    next_scr[1] = top
    next_scr[0] = below
    act_scr[1] = act.astype(BF)
    act_scr[0] = tanh_of(states_ref[0]).astype(BF)
    adjoint_ref[0] = (guess_ref[...].astype(F32) + widened(low_own, high_own)).astype(BF)
    adjoint_ref[1] = below
    lent_ref[...] = next_scr[core]
    own_ref[...] = next_scr[1 - core]
    act_ref[...] = act_scr[1 - core]


def gradient_of(act, field, stack_ref):
    write_stack(field, stack_ref)
    contract = (((1,), (1,)), ((), ()))
    return STEP * lax.dot_general(act, stack_ref[...], contract, preferred_element_type=F32)


def own_kernel(adjoint_ref, own_ref, act_ref, other_ref, out_hbm, grad_ref, other_act_ref, stack_ref, sem):
    copy = pltpu.make_async_copy(adjoint_ref, out_hbm, sem)
    copy.start()
    other_act_ref[...] = tanh_of(other_ref[...]).astype(BF)
    grad_ref[...] = gradient_of(act_ref[...], own_ref[...], stack_ref)
    copy.wait()


def other_kernel(came_ref, other_act_ref, grad_ref, share_ref, stack_ref):
    grad = grad_ref[...] + gradient_of(other_act_ref[...], came_ref[...], stack_ref)
    share_ref[...] = grad.reshape(2 * ZS, 8, TAPS * CH).astype(BF)


def total_kernel(came_ref, grad_ref):
    for l in range(2):
        total = came_ref[1 - l].astype(F32)
        for z in range(1, ZS):
            total += came_ref[2 * z + 1 - l].astype(F32)
        grad_ref[l] = total


def call(body, outs, scratch=(), flops=10**6, vmem=6, in_specs=None, out_specs=None):
    outs = [jax.ShapeDtypeStruct(s, d) for s, d in outs]
    extra = {} if in_specs is None else {"in_specs": in_specs}
    if out_specs is not None:
        extra["out_specs"] = out_specs
    return pl.pallas_call(
        body,
        out_shape=outs[0] if len(outs) == 1 else outs,
        scratch_shapes=list(scratch),
        compiler_params=pltpu.CompilerParams(vmem_limit_bytes=vmem << 20),
        cost_estimate=pl.CostEstimate(flops=flops, bytes_accessed=1 << 20, transcendentals=0),
        **extra,
    )


WIDTH = CELLS + CH
FIELD = (CH, PIX)
STACK = pltpu.VMEM((TAPS * CH, PIX), BF)
ANY = pl.BlockSpec(memory_space=pl.ANY)
prep = call(prep_kernel, [((CH, CH), BF), (FIELD, BF), ((2,) + FIELD, BF), (FIELD, BF)])
fine = call(fine_kernel, [(FIELD, BF), ((GROUP, CH, WIDTH), BF)], [STACK], 10**9, 16)
group_of = call(group_kernel, [((GROUPS, CH, WIDTH), BF)])
correct = call(
    correct_kernel,
    [((2,) + FIELD, BF), (FIELD, BF), (FIELD, BF), (FIELD, BF)],
    [
        pltpu.VMEM((GROUP, CH, WIDTH), BF),
        pltpu.VMEM(FIELD, BF),
        pltpu.VMEM(FIELD, BF),
        pltpu.VMEM((2,) + FIELD, BF),
        pltpu.VMEM((CH, TAPS * CH), BF),
        STACK,
        pltpu.VMEM((2,) + FIELD, BF),
        pltpu.VMEM((2,) + FIELD, BF),
        pltpu.SemaphoreType.DMA((5,)),
    ],
    10**9,
    20,
    [VMEM] + [ANY] * 5,
)
own_part = call(
    own_kernel,
    [((2,) + FIELD, BF), ((CH, TAPS * CH), F32), (FIELD, BF)],
    [STACK, pltpu.SemaphoreType.DMA(())],
    10**9,
    12,
    [VMEM] * 4,
    [ANY, VMEM, VMEM],
)
other_part = call(other_kernel, [((2 * ZS, 8, TAPS * CH), BF)], [STACK], 10**9, 12)
total_of = call(total_kernel, [((2, 8, TAPS * CH), F32)])


def per_device(states, filters, guess, terminal):
    states, guess, terminal = states[:, 0], guess[:, 0], terminal[0]
    near_groups = [[k * GROUP + j for j in range(GROUP)] for k in range(GROUPS)]
    far_groups = [[k * GROUP + j for k in range(GROUPS)] for j in range(GROUP)]

    def exchange(a, axis, groups):
        return lax.all_to_all(a, axis, 0, 0, axis_index_groups=groups)

    above = lax.ppermute(guess[0], "layer", [(i + 1, i) for i in range(GROUP * GROUPS - 1)])
    matrix, ending, kept, lent = prep(filters, terminal, states)
    swap = [(i ^ 1, i) for i in range(2 * ZS)]
    other = lax.ppermute(lent, "dp", swap)
    above, other = lax.optimization_barrier((above, other))
    top, pack = fine(above, ending, guess[0], kept, filters, matrix)
    packs = exchange(pack, "layer", near_groups)
    groups = exchange(group_of(packs), "layer", far_groups)
    fresh, own, lent, act = correct(groups, packs, top, guess, states, filters)
    came = lax.ppermute(lent, "dp", swap)
    adjoint, grad, other_act = own_part(fresh, own, act, other)
    shares = lax.all_to_all(other_part(came, other_act, grad), "dp", 0, 0)
    return adjoint[:, None], total_of(shares)


def solution(mesh):
    return jax.shard_map(
        per_device,
        mesh=mesh,
        in_specs=(
            P("layer", "dp", None, None),
            P("layer", None, None),
            P("layer", "dp", None, None),
            P("dp", None, None),
        ),
        out_specs=(P("layer", "dp", None, None), P("layer", "dp", None)),
        check_vma=False,
    )
```

```python
import jax
import jax.numpy as jnp
from jax import lax
from jax.experimental import pallas as pl
from jax.experimental.pallas import tpu as pltpu
from jax.sharding import PartitionSpec as P


STEP = 0.0625
KEEP = 1.0 - STEP
SIDE, PIX, CH, TAPS = 32, 1024, 128, 9
HALF = SIDE // 2
CELLS = HALF * HALF
GROUP, GROUPS, ZS = 8, 4, 8
BF, F32 = jnp.bfloat16, jnp.float32
EXACT = lax.Precision.HIGHEST
VMEM = pl.BlockSpec(memory_space=pltpu.VMEM)


def dot(a, b, precision=None):
    return jnp.dot(a, b, preferred_element_type=F32, precision=precision)


def split(a):
    high = a.astype(BF)
    return high, (a - high.astype(F32)).astype(BF)


def write_stack(field, stack_ref):
    lane = lax.broadcasted_iota(jnp.int32, (1, PIX), 1)
    col = lane & (SIDE - 1)
    first, last = (col != 0).astype(BF), (col != SIDE - 1).astype(BF)
    top, bottom = (lane >= SIDE).astype(BF), (lane < PIX - SIDE).astype(BF)
    columns = (
        pltpu.roll(field, PIX - 1, 1) * last,
        field,
        pltpu.roll(field, 1, 1) * first,
    )
    for c, moved in enumerate(columns):
        rows = (
            pltpu.roll(moved, PIX - SIDE, 1) * bottom,
            moved,
            pltpu.roll(moved, SIDE, 1) * top,
        )
        for a, piece in enumerate(rows):
            t = 3 * a + c
            stack_ref[t * CH : (t + 1) * CH, :] = piece


def pool_matrix():
    pixel = lax.broadcasted_iota(jnp.int32, (PIX, CELLS), 0)
    cell = lax.broadcasted_iota(jnp.int32, (PIX, CELLS), 1)
    square = ((pixel >> 6) << 4) + ((pixel & (SIDE - 1)) >> 1)
    return square == cell


def spread_matrix():
    cell = lax.broadcasted_iota(jnp.int32, (CELLS, PIX), 0)
    pixel = lax.broadcasted_iota(jnp.int32, (CELLS, PIX), 1)
    square = ((pixel >> 6) << 4) + ((pixel & (SIDE - 1)) >> 1)
    return (square == cell).astype(F32).astype(BF)


def rounded(part):
    row = lax.broadcasted_iota(jnp.int32, (CH, CH), 0).astype(F32)
    col = lax.broadcasted_iota(jnp.int32, (CH, CH), 1).astype(F32)
    place = row * 0.7548776662 + col * 0.5698402910
    offset = place - jnp.floor(place) - 0.5
    return (part + part * offset * 0.00546875).astype(BF)


def times(left, right):
    left_high, left_low = split(left)
    right_high, right_low = split(right)
    return dot(left_high, right_high) + dot(left_high, right_low) + dot(left_low, right_high)


def times_part(part, right):
    high, low = split(right)
    return dot(part, high) + dot(part, low)


def tanh_of(state):
    return jnp.tanh(state.astype(F32))


def slope_of(act):
    return STEP * (1.0 - act * act)


def matrix_kernel(filters_ref, matrix_ref):
    total = filters_ref[0, :, 0:CH].astype(F32)
    for t in range(1, TAPS):
        total += filters_ref[0, :, t * CH : (t + 1) * CH].astype(F32)
    total *= STEP
    part = rounded((2.0 * KEEP) * total + dot(total, total, EXACT))
    for j in range(GROUP):
        matrix_ref[j] = part


def prep_kernel(terminal_ref, states_ref, ending_ref, kept_ref):
    ending_ref[...] = terminal_ref[...]
    kept_ref[...] = states_ref[...]


def fine_kernel(
    above_ref, terminal_ref, guess_ref, states_ref, filters_ref, top_ref, pack_ref, stack_ref
):
    last = lax.axis_index("layer") == GROUP * GROUPS - 1
    top = jnp.where(last, terminal_ref[...].astype(F32), above_ref[...].astype(F32))
    top_ref[...] = top.astype(BF)
    write_stack(top.astype(BF), stack_ref)
    below = KEEP * top + slope_of(tanh_of(states_ref[1])) * dot(filters_ref[1], stack_ref[...])
    below = below.astype(BF)
    write_stack(below, stack_ref)
    moved = slope_of(tanh_of(states_ref[0])) * dot(filters_ref[0], stack_ref[...])
    residual = KEEP * below.astype(F32) + moved - guess_ref[...].astype(F32)
    high, low = split(residual)
    pool = jnp.where(pool_matrix(), 0.25, 0.0).astype(BF)
    coarse = (dot(high, pool) + dot(low, pool)).astype(BF)
    for j in range(GROUP):
        pack_ref[j] = coarse


def paired(scale, fields, parts):
    near, far, left, right = fields[::2], fields[1::2], parts[::2], parts[1::2]
    joint = [a + scale * b + times(part, b) for a, b, part in zip(near, far, left)]
    mixed = [scale * (a + b) + times(a, b) for a, b in zip(left, right)]
    return scale * scale, joint, mixed


def group_kernel(coarse_ref, part_ref, pack_ref):
    scale = KEEP**2
    coarse = [coarse_ref[j] for j in range(GROUP)]
    part = [part_ref[j] for j in range(GROUP)]
    fields, parts = [], []
    for j in range(0, GROUP, 2):
        fields.append(coarse[j].astype(F32) + scale * coarse[j + 1].astype(F32) + dot(part[j], coarse[j + 1]))
        parts.append(scale * (part[j].astype(F32) + part[j + 1].astype(F32)) + dot(part[j], part[j + 1]))
    scale *= scale
    while len(fields) > 1:
        scale, fields, parts = paired(scale, fields, parts)
    value, group = fields[0].astype(BF), rounded(parts[0])
    for j in range(GROUPS):
        pack_ref[j, :, :CELLS] = value
        pack_ref[j, :, CELLS:] = group


def applied(local, error):
    return local[0] + local[1] * error + times(local[2], error)


def upper_error(groups_ref, at):
    scale = KEEP ** (2 * GROUP)
    pairs = []
    for a in range(0, GROUPS, 2):
        on = [(a + i > at).astype(F32) for i in range(2)]
        hold = [jnp.where(a + i > at, scale, 1.0) for i in range(2)]
        values = [groups_ref[a + i, :, :CELLS] for i in range(2)]
        parts = [groups_ref[a + i, :, CELLS:] for i in range(2)]
        mixed = hold[0] * values[1].astype(F32) + on[0] * dot(parts[0], values[1])
        field = on[0] * values[0].astype(F32) + on[1] * mixed
        crossed = (hold[0] * on[1]) * parts[1].astype(F32) + (hold[1] * on[0]) * parts[0].astype(F32)
        crossed += (on[0] * on[1]) * dot(parts[0], parts[1])
        pairs.append((field, hold[0] * hold[1], crossed))
    return applied(pairs[0], pairs[1][0])


def suffix_maps(coarse_ref, part_ref, first, last):
    scale = KEEP**2
    coarse = {j: coarse_ref[j] for j in range(first, last + 1)}
    part = {j: part_ref[j] for j in range(first, last + 1)}
    field, hold, crossed = coarse[last].astype(F32), scale, part[last].astype(F32)
    maps = {last: (field, hold, crossed)}
    for j in range(last - 1, first - 1, -1):
        field = coarse[j].astype(F32) + scale * field + times_part(part[j], field)
        crossed = scale * crossed + hold * part[j].astype(F32) + times_part(part[j], crossed)
        hold *= scale
        maps[j] = (field, hold, crossed)
    return maps


def picked(maps, default, at):
    for j, local in maps.items():
        default = tuple(jnp.where(at == j, a, b) for a, b in zip(local, default))
    return default


def correct_kernel(
    groups_ref, coarse_ref, part_ref, top_ref, guess_ref, states_ref, filters_ref,
    adjoint_ref, own_ref, lent_ref, act_ref,
    stack_ref, next_scr, act_scr,
):
    layer = lax.axis_index("layer")
    core = lax.axis_index("dp") % 2
    place, at = layer % GROUP, layer // GROUP
    half = GROUP // 2
    low, high = suffix_maps(coarse_ref, part_ref, 0, half - 1), suffix_maps(coarse_ref, part_ref, half, GROUP - 1)
    nil = (jnp.zeros((CH, CELLS), F32), 1.0, jnp.zeros((CH, CH), F32))
    low_own = picked(low, nil, place)
    low_upper = picked({j - 1: low[j] for j in range(1, half)}, nil, place)
    high_own = picked({j: high[j] for j in range(half + 1, GROUP)}, high[half], place)
    high_upper = picked({j - 1: high[j] for j in range(half + 1, GROUP)}, high[half], place)
    high_upper = picked({GROUP - 1: nil}, high_upper, place)
    far = upper_error(groups_ref, at)
    spread = spread_matrix()

    def widened(near, beyond):
        high_part, low_part = split(applied(near, applied(beyond, far)))
        return dot(high_part, spread) + dot(low_part, spread)

    top = (top_ref[...].astype(F32) + widened(low_upper, high_upper)).astype(BF)
    write_stack(top, stack_ref)
    act = tanh_of(states_ref[1])
    below = KEEP * top.astype(F32) + slope_of(act) * dot(filters_ref[1], stack_ref[...])
    below = below.astype(BF)
    next_scr[1] = top
    next_scr[0] = below
    act_scr[1] = act.astype(BF)
    act_scr[0] = tanh_of(states_ref[0]).astype(BF)
    adjoint_ref[0] = (guess_ref[0].astype(F32) + widened(low_own, high_own)).astype(BF)
    adjoint_ref[1] = below
    lent_ref[0] = next_scr[core]
    lent_ref[1] = act_scr[core]
    own_ref[...] = next_scr[1 - core]
    act_ref[...] = act_scr[1 - core]


def gradient_of(act, field, stack_ref):
    write_stack(field, stack_ref)
    contract = (((1,), (1,)), ((), ()))
    return STEP * lax.dot_general(act, stack_ref[...], contract, preferred_element_type=F32)


def own_kernel(adjoint_ref, own_ref, act_ref, out_hbm, grad_ref, stack_ref, sem):
    copy = pltpu.make_async_copy(adjoint_ref, out_hbm, sem)
    copy.start()
    grad_ref[...] = gradient_of(act_ref[...], own_ref[...], stack_ref)
    copy.wait()


def other_kernel(came_ref, grad_ref, share_ref, stack_ref):
    grad = grad_ref[...] + gradient_of(came_ref[1], came_ref[0], stack_ref)
    share_ref[...] = grad.reshape(2 * ZS, 8, TAPS * CH).astype(BF)


def total_kernel(came_ref, grad_ref):
    for l in range(2):
        total = came_ref[1 - l].astype(F32)
        for z in range(1, ZS):
            total += came_ref[2 * z + 1 - l].astype(F32)
        grad_ref[l] = total


def call(body, outs, scratch=(), flops=10**6, vmem=6, in_specs=None, out_specs=None):
    outs = [jax.ShapeDtypeStruct(s, d) for s, d in outs]
    extra = {} if in_specs is None else {"in_specs": in_specs}
    if out_specs is not None:
        extra["out_specs"] = out_specs
    return pl.pallas_call(
        body,
        out_shape=outs[0] if len(outs) == 1 else outs,
        scratch_shapes=list(scratch),
        compiler_params=pltpu.CompilerParams(vmem_limit_bytes=vmem << 20),
        cost_estimate=pl.CostEstimate(flops=flops, bytes_accessed=1 << 20, transcendentals=0),
        **extra,
    )


WIDTH = CELLS + CH
FIELD = (CH, PIX)
STACK = pltpu.VMEM((TAPS * CH, PIX), BF)
ANY = pl.BlockSpec(memory_space=pl.ANY)
matrix_of = call(matrix_kernel, [((GROUP, CH, CH), BF)])
prep = call(prep_kernel, [(FIELD, BF), ((2,) + FIELD, BF)])
fine = call(fine_kernel, [(FIELD, BF), ((GROUP, CH, CELLS), BF)], [STACK], 10**9, 16)
group_of = call(group_kernel, [((GROUPS, CH, WIDTH), BF)])
correct = call(
    correct_kernel,
    [((2,) + FIELD, BF), (FIELD, BF), ((2,) + FIELD, BF), (FIELD, BF)],
    [
        STACK,
        pltpu.VMEM((2,) + FIELD, BF),
        pltpu.VMEM((2,) + FIELD, BF),
    ],
    10**9,
    16,
)
own_part = call(
    own_kernel,
    [((2,) + FIELD, BF), ((CH, TAPS * CH), F32)],
    [STACK, pltpu.SemaphoreType.DMA(())],
    10**9,
    12,
    [VMEM] * 3,
    [ANY, VMEM],
)
other_part = call(other_kernel, [((2 * ZS, 8, TAPS * CH), BF)], [STACK], 10**9, 12)
total_of = call(total_kernel, [((2, 8, TAPS * CH), F32)])


def iterate(states, filters, guess, terminal):
    states, guess, terminal = states[:, 0], guess[:, 0], terminal[0]
    near_groups = [[k * GROUP + j for j in range(GROUP)] for k in range(GROUPS)]
    far_groups = [[k * GROUP + j for k in range(GROUPS)] for j in range(GROUP)]

    def exchange(a, axis, groups):
        return lax.all_to_all(a, axis, 0, 0, axis_index_groups=groups)

    above = lax.ppermute(guess[0], "layer", [(i + 1, i) for i in range(GROUP * GROUPS - 1)])
    matrix = matrix_of(filters)
    parts = exchange(matrix, "layer", near_groups)
    ending, kept = prep(terminal, states)
    swap = [(i ^ 1, i) for i in range(2 * ZS)]
    top, pack = fine(above, ending, guess[0], kept, filters)
    coarses = exchange(pack, "layer", near_groups)
    groups = exchange(group_of(coarses, parts), "layer", far_groups)
    fresh, own, lent, act = correct(groups, coarses, parts, top, guess, states, filters)
    came = lax.ppermute(lent, "dp", swap)
    adjoint, grad = own_part(fresh, own, act)
    shares = lax.all_to_all(other_part(came, grad), "dp", 0, 0)
    return adjoint[:, None], total_of(shares)


def solution(mesh):
    return jax.shard_map(
        iterate,
        mesh=mesh,
        in_specs=(
            P("layer", "dp", None, None),
            P("layer", None, None),
            P("layer", "dp", None, None),
            P("dp", None, None),
        ),
        out_specs=(P("layer", "dp", None, None), P("layer", "dp", None)),
        check_vma=False,
    )
```

```python
import jax
import jax.numpy as jnp
from jax import lax
from jax.experimental import pallas as pl
from jax.experimental.pallas import tpu as pltpu
from jax.sharding import PartitionSpec as P


STEP = 0.0625
KEEP = 1.0 - STEP
SIDE, PIX, CH, TAPS = 32, 1024, 128, 9
HALF = SIDE // 2
CELLS = HALF * HALF
GROUP, GROUPS, ZS = 8, 4, 8
BF, F32 = jnp.bfloat16, jnp.float32
EXACT = lax.Precision.HIGHEST
VMEM = pl.BlockSpec(memory_space=pltpu.VMEM)


def dot(a, b, precision=None):
    return jnp.dot(a, b, preferred_element_type=F32, precision=precision)


def split(a):
    high = a.astype(BF)
    return high, (a - high.astype(F32)).astype(BF)


def write_stack(field, stack_ref):
    lane = lax.broadcasted_iota(jnp.int32, (1, PIX), 1)
    col = lane & (SIDE - 1)
    first, last = (col != 0).astype(BF), (col != SIDE - 1).astype(BF)
    top, bottom = (lane >= SIDE).astype(BF), (lane < PIX - SIDE).astype(BF)
    columns = (
        pltpu.roll(field, PIX - 1, 1) * last,
        field,
        pltpu.roll(field, 1, 1) * first,
    )
    for c, moved in enumerate(columns):
        rows = (
            pltpu.roll(moved, PIX - SIDE, 1) * bottom,
            moved,
            pltpu.roll(moved, SIDE, 1) * top,
        )
        for a, piece in enumerate(rows):
            t = 3 * a + c
            stack_ref[t * CH : (t + 1) * CH, :] = piece


def pool_matrix():
    pixel = lax.broadcasted_iota(jnp.int32, (PIX, CELLS), 0)
    cell = lax.broadcasted_iota(jnp.int32, (PIX, CELLS), 1)
    square = ((pixel >> 6) << 4) + ((pixel & (SIDE - 1)) >> 1)
    return square == cell


def spread_matrix():
    cell = lax.broadcasted_iota(jnp.int32, (CELLS, PIX), 0)
    pixel = lax.broadcasted_iota(jnp.int32, (CELLS, PIX), 1)
    square = ((pixel >> 6) << 4) + ((pixel & (SIDE - 1)) >> 1)
    return (square == cell).astype(F32).astype(BF)


def rounded(part):
    row = lax.broadcasted_iota(jnp.int32, (CH, CH), 0).astype(F32)
    col = lax.broadcasted_iota(jnp.int32, (CH, CH), 1).astype(F32)
    place = row * 0.7548776662 + col * 0.5698402910
    offset = place - jnp.floor(place) - 0.5
    return (part + part * offset * 0.00546875).astype(BF)


def times(left, right):
    left_high, left_low = split(left)
    right_high, right_low = split(right)
    return dot(left_high, right_high) + dot(left_high, right_low) + dot(left_low, right_high)


def times_part(part, right):
    high, low = split(right)
    return dot(part, high) + dot(part, low)


def tanh_of(state):
    return jnp.tanh(state.astype(F32))


def slope_of(act):
    return STEP * (1.0 - act * act)


def matrix_kernel(filters_ref, matrix_ref):
    total = filters_ref[0, :, 0:CH].astype(F32)
    for t in range(1, TAPS):
        total += filters_ref[0, :, t * CH : (t + 1) * CH].astype(F32)
    total *= STEP
    part = rounded((2.0 * KEEP) * total + dot(total, total, EXACT))
    for j in range(GROUP):
        matrix_ref[j] = part


def prep_kernel(terminal_ref, states_ref, ending_ref, kept_ref):
    ending_ref[...] = terminal_ref[...]
    kept_ref[...] = states_ref[...]


def fine_kernel(
    above_ref, terminal_ref, guess_ref, states_ref, filters_ref, top_ref, pack_ref, stack_ref
):
    last = lax.axis_index("layer") == GROUP * GROUPS - 1
    top = jnp.where(last, terminal_ref[...].astype(F32), above_ref[...].astype(F32))
    top_ref[...] = top.astype(BF)
    write_stack(top.astype(BF), stack_ref)
    below = KEEP * top + slope_of(tanh_of(states_ref[1])) * dot(filters_ref[1], stack_ref[...])
    below = below.astype(BF)
    write_stack(below, stack_ref)
    moved = slope_of(tanh_of(states_ref[0])) * dot(filters_ref[0], stack_ref[...])
    residual = KEEP * below.astype(F32) + moved - guess_ref[...].astype(F32)
    pool = jnp.where(pool_matrix(), 0.25, 0.0).astype(BF)
    coarse = dot(residual.astype(BF), pool).astype(BF)
    for j in range(GROUP):
        pack_ref[j] = coarse


def paired(scale, fields, parts):
    near, far, left, right = fields[::2], fields[1::2], parts[::2], parts[1::2]
    joint = [a + scale * b + times(part, b) for a, b, part in zip(near, far, left)]
    mixed = [scale * (a + b) + times(a, b) for a, b in zip(left, right)]
    return scale * scale, joint, mixed


def group_kernel(coarse_ref, part_ref, pack_ref):
    scale = KEEP**2
    coarse = [coarse_ref[j] for j in range(GROUP)]
    part = [part_ref[j] for j in range(GROUP)]
    fields, parts = [], []
    for j in range(0, GROUP, 2):
        fields.append(coarse[j].astype(F32) + scale * coarse[j + 1].astype(F32) + dot(part[j], coarse[j + 1]))
        parts.append(scale * (part[j].astype(F32) + part[j + 1].astype(F32)) + dot(part[j], part[j + 1]))
    scale *= scale
    while len(fields) > 1:
        scale, fields, parts = paired(scale, fields, parts)
    value, group = fields[0].astype(BF), rounded(parts[0])
    for j in range(GROUPS):
        pack_ref[j, :, :CELLS] = value
        pack_ref[j, :, CELLS:] = group


def applied(local, error):
    return local[0] + local[1] * error + times(local[2], error)


def upper_error(groups_ref, at):
    scale = KEEP ** (2 * GROUP)
    pairs = []
    for a in range(0, GROUPS, 2):
        on = [(a + i > at).astype(F32) for i in range(2)]
        hold = [jnp.where(a + i > at, scale, 1.0) for i in range(2)]
        values = [groups_ref[a + i, :, :CELLS] for i in range(2)]
        parts = [groups_ref[a + i, :, CELLS:] for i in range(2)]
        mixed = hold[0] * values[1].astype(F32) + on[0] * dot(parts[0], values[1])
        field = on[0] * values[0].astype(F32) + on[1] * mixed
        crossed = (hold[0] * on[1]) * parts[1].astype(F32) + (hold[1] * on[0]) * parts[0].astype(F32)
        crossed += (on[0] * on[1]) * dot(parts[0], parts[1])
        pairs.append((field, hold[0] * hold[1], crossed))
    return applied(pairs[0], pairs[1][0])


def suffix_maps(coarse_ref, part_ref, first, last):
    scale = KEEP**2
    coarse = {j: coarse_ref[j] for j in range(first, last + 1)}
    part = {j: part_ref[j] for j in range(first, last + 1)}
    field, hold, crossed = coarse[last].astype(F32), scale, part[last].astype(F32)
    maps = {last: (field, hold, crossed)}
    for j in range(last - 1, first - 1, -1):
        field = coarse[j].astype(F32) + scale * field + times_part(part[j], field)
        crossed = scale * crossed + hold * part[j].astype(F32) + times_part(part[j], crossed)
        hold *= scale
        maps[j] = (field, hold, crossed)
    return maps


def picked(maps, default, at):
    for j, local in maps.items():
        default = tuple(jnp.where(at == j, a, b) for a, b in zip(local, default))
    return default


def field_kernel(states_ref, top_ref, act_ref, slope_ref, spread_ref):
    act = tanh_of(states_ref[1])
    slope_ref[...] = slope_of(act)
    act_ref[1] = act.astype(BF)
    act_ref[0] = tanh_of(states_ref[0]).astype(BF)
    spread_ref[...] = spread_matrix()


def correct_kernel(
    groups_ref, coarse_ref, part_ref, top_ref, guess_ref, fields_ref, slope_ref, spread_ref, filters_ref,
    adjoint_ref, own_ref, lent_ref, act_ref,
    stack_ref, next_scr,
):
    layer = lax.axis_index("layer")
    core = lax.axis_index("dp") % 2
    place, at = layer % GROUP, layer // GROUP
    half = GROUP // 2
    low, high = suffix_maps(coarse_ref, part_ref, 0, half - 1), suffix_maps(coarse_ref, part_ref, half, GROUP - 1)
    nil = (jnp.zeros((CH, CELLS), F32), 1.0, jnp.zeros((CH, CH), F32))
    low_own = picked(low, nil, place)
    low_upper = picked({j - 1: low[j] for j in range(1, half)}, nil, place)
    high_own = picked({j: high[j] for j in range(half + 1, GROUP)}, high[half], place)
    high_upper = picked({j - 1: high[j] for j in range(half + 1, GROUP)}, high[half], place)
    high_upper = picked({GROUP - 1: nil}, high_upper, place)
    far = upper_error(groups_ref, at)
    spread = spread_ref[...]

    def widened(near, beyond):
        high_part, low_part = split(applied(near, applied(beyond, far)))
        return dot(high_part, spread) + dot(low_part, spread)

    top = (top_ref[...].astype(F32) + widened(low_upper, high_upper)).astype(BF)
    write_stack(top, stack_ref)
    below = KEEP * top.astype(F32) + slope_ref[...] * dot(filters_ref[1], stack_ref[...])
    below = below.astype(BF)
    next_scr[1] = top
    next_scr[0] = below
    adjoint_ref[0] = (guess_ref[0].astype(F32) + widened(low_own, high_own)).astype(BF)
    adjoint_ref[1] = below
    lent_ref[0] = next_scr[core]
    lent_ref[1] = fields_ref[core]
    own_ref[...] = next_scr[1 - core]
    act_ref[...] = fields_ref[1 - core]


def gradient_of(act, field, stack_ref):
    write_stack(field, stack_ref)
    contract = (((1,), (1,)), ((), ()))
    return STEP * lax.dot_general(act, stack_ref[...], contract, preferred_element_type=F32)


def own_kernel(adjoint_ref, own_ref, act_ref, out_hbm, grad_ref, stack_ref, sem):
    copy = pltpu.make_async_copy(adjoint_ref, out_hbm, sem)
    copy.start()
    grad_ref[...] = gradient_of(act_ref[...], own_ref[...], stack_ref)
    copy.wait()


def other_kernel(came_ref, grad_ref, share_ref, stack_ref):
    grad = grad_ref[...] + gradient_of(came_ref[1], came_ref[0], stack_ref)
    share_ref[...] = grad.reshape(2 * ZS, 8, TAPS * CH).astype(BF)


def total_kernel(came_ref, grad_ref):
    for l in range(2):
        total = came_ref[1 - l].astype(F32)
        for z in range(1, ZS):
            total += came_ref[2 * z + 1 - l].astype(F32)
        grad_ref[l] = total


def call(body, outs, scratch=(), flops=10**6, vmem=6, in_specs=None, out_specs=None):
    outs = [jax.ShapeDtypeStruct(s, d) for s, d in outs]
    extra = {} if in_specs is None else {"in_specs": in_specs}
    if out_specs is not None:
        extra["out_specs"] = out_specs
    return pl.pallas_call(
        body,
        out_shape=outs[0] if len(outs) == 1 else outs,
        scratch_shapes=list(scratch),
        compiler_params=pltpu.CompilerParams(vmem_limit_bytes=vmem << 20),
        cost_estimate=pl.CostEstimate(flops=flops, bytes_accessed=1 << 20, transcendentals=0),
        **extra,
    )


WIDTH = CELLS + CH
FIELD = (CH, PIX)
STACK = pltpu.VMEM((TAPS * CH, PIX), BF)
ANY = pl.BlockSpec(memory_space=pl.ANY)
matrix_of = call(matrix_kernel, [((GROUP, CH, CH), BF)])
prep = call(prep_kernel, [(FIELD, BF), ((2,) + FIELD, BF)])
fine = call(fine_kernel, [(FIELD, BF), ((GROUP, CH, CELLS), BF)], [STACK], 10**9, 16)
group_of = call(group_kernel, [((GROUPS, CH, WIDTH), BF)])
field_of = call(field_kernel, [((2,) + FIELD, BF), (FIELD, F32), ((CELLS, PIX), BF)], vmem=8)
correct = call(
    correct_kernel,
    [((2,) + FIELD, BF), (FIELD, BF), ((2,) + FIELD, BF), (FIELD, BF)],
    [
        STACK,
        pltpu.VMEM((2,) + FIELD, BF),
    ],
    10**9,
    16,
)
own_part = call(
    own_kernel,
    [((2,) + FIELD, BF), ((CH, TAPS * CH), F32)],
    [STACK, pltpu.SemaphoreType.DMA(())],
    10**9,
    12,
    [VMEM] * 3,
    [ANY, VMEM],
)
other_part = call(other_kernel, [((2 * ZS, 8, TAPS * CH), BF)], [STACK], 10**9, 12)
total_of = call(total_kernel, [((2, 8, TAPS * CH), F32)])


def iterate(states, filters, guess, terminal):
    states, guess, terminal = states[:, 0], guess[:, 0], terminal[0]
    near_groups = [[k * GROUP + j for j in range(GROUP)] for k in range(GROUPS)]
    far_groups = [[k * GROUP + j for k in range(GROUPS)] for j in range(GROUP)]

    def exchange(a, axis, groups):
        return lax.all_to_all(a, axis, 0, 0, axis_index_groups=groups)

    above = lax.ppermute(guess[0], "layer", [(i + 1, i) for i in range(GROUP * GROUPS - 1)])
    matrix = matrix_of(filters)
    parts = exchange(matrix, "layer", near_groups)
    ending, kept = prep(terminal, states)
    swap = [(i ^ 1, i) for i in range(2 * ZS)]
    top, pack = fine(above, ending, guess[0], kept, filters)
    fields, slope, spread = field_of(kept, top)
    coarses = exchange(pack, "layer", near_groups)
    groups = exchange(group_of(coarses, parts), "layer", far_groups)
    fresh, own, lent, act = correct(groups, coarses, parts, top, guess, fields, slope, spread, filters)
    came = lax.ppermute(lent, "dp", swap)
    adjoint, grad = own_part(fresh, own, act)
    shares = lax.all_to_all(other_part(came, grad), "dp", 0, 0)
    return adjoint[:, None], total_of(shares)


def solution(mesh):
    return jax.shard_map(
        iterate,
        mesh=mesh,
        in_specs=(
            P("layer", "dp", None, None),
            P("layer", None, None),
            P("layer", "dp", None, None),
            P("dp", None, None),
        ),
        out_specs=(P("layer", "dp", None, None), P("layer", "dp", None)),
        check_vma=False,
    )
```
